32 devices in a mesh: seq: 8 (over z, x), dp: 2 (over y), head: 2 (over core).
Axes of the slice: x: 2, y: 2, z: 4, core: 2. Of those that a mesh axis runs over, the one named last changes fastest.
Arguments:
- queries: bfloat16 [2, 1024, 2048], P('dp', 'seq', 'head'), may hold values from -5 to 5
- keys: bfloat16 [2, 1024, 512], P('dp', 'seq', 'head'), may hold values from -5 to 5
- values: bfloat16 [2, 1024, 512], P('dp', 'seq', 'head'), may hold values from -4 to 4
- query_tangent: bfloat16 [2, 1024, 2048], P('dp', 'seq', 'head'), may hold values from -4 to 4
- key_tangent: bfloat16 [2, 1024, 512], P('dp', 'seq', 'head'), may hold values from -4 to 4
- value_tangent: bfloat16 [2, 1024, 512], P('dp', 'seq', 'head'), may hold values from -4 to 4
- lengths: int32 [2, 9], P('dp'), may hold values from 0 to 256, as said below
- out_weight: bfloat16 [2048, 4096], P('head'), may hold values from -0.125 to 0.125
- cotangent: bfloat16 [2, 1024, 4096], P('dp', 'seq'), may hold values from -0.1875 to 0.1875
Outputs:
- layer_tangent: bfloat16 [2, 1024, 4096], P('dp', 'seq', 'head')
- weight_hvp: float32 [4096, 2048], P(('seq', 'dp'), 'head')
The draws below stay inside these ranges and needn't reach their ends.
Inputs may be any that keep to these rules, and one draw needn't show every extreme that they name: `lengths`: each row sums to 1024; a length may be 0; in every row some document has exactly 256 tokens.
All inputs are finite; a program needn't handle non-finite values.
Results may differ from the reference program's by a relative error of at most 0.014.
Values may be sent and summed in bfloat16 or wider, within the bound.
No kernel may reach another device: no remote copies, remote signals or barrier semaphores. Data moves between devices by JAX's collectives and lax.ppermute only.
A program may use at most 128 MiB of HBM per device.

```python
import jax
import jax.numpy as jnp
from jax import lax

D = 4096
HEADS = 16
KV_HEADS = 4
HEAD_DIM = 128
DOC_SHARDS = 2
SEQLEN = 1024
BATCH = 2
DOCMAX = 256
N_SEQ = 8


def doc_layout(key):
    base = jax.random.fold_in(key, 7)
    key_parts = jax.random.split(base, 3)
    group_count = N_SEQ // DOC_SHARDS
    offsets = jax.random.randint(key_parts[0], (BATCH,), 0, DOCMAX)
    spans = jnp.concatenate([jnp.full((BATCH, group_count - 1), DOCMAX, jnp.int32), (DOCMAX - offsets)[:, None].astype(jnp.int32)], axis=1)
    cuts = jax.random.randint(key_parts[1], (BATCH, group_count, DOC_SHARDS - 1), 0, spans[:, :, None] + 1)
    forced = jax.random.randint(key_parts[2], (BATCH,), 0, group_count - 1)
    chosen = jnp.arange(group_count, dtype=jnp.int32)[None, :] == forced[:, None]
    cuts = jnp.where(chosen[:, :, None], 0, cuts)
    cuts = jnp.sort(cuts, axis=-1)
    bounds = jnp.concatenate([jnp.zeros((BATCH, group_count, 1), jnp.int32), cuts.astype(jnp.int32), spans[:, :, None]], axis=-1)
    pieces = bounds[:, :, 1:] - bounds[:, :, :-1]
    lengths = jnp.concatenate([offsets[:, None].astype(jnp.int32), pieces.reshape(BATCH, group_count * DOC_SHARDS)], axis=1)
    return lengths.astype(jnp.int32)


def draw_lengths(key, part):
    return doc_layout(key)


def draw_queries(key, part):
    shape = (BATCH, SEQLEN, HEADS * HEAD_DIM)
    field = jnp.clip(jax.random.normal(jax.random.fold_in(key, 21), shape, jnp.float32), -4.0, 4.0)
    return field.astype(jnp.bfloat16)


def draw_keys(key, part):
    shape = (BATCH, SEQLEN, KV_HEADS * HEAD_DIM)
    field = jnp.clip(jax.random.normal(jax.random.fold_in(key, 22), shape, jnp.float32), -4.0, 4.0)
    return field.astype(jnp.bfloat16)


def raised(drawn, rng, source, target, blocks, factor):
    owner, partner = [(jnp.arange(drawn.shape[dim]) // (drawn.shape[dim] // blocks)).reshape([-1 if axis == dim else 1 for axis in range(drawn.ndim)]) for dim in (source, target)]
    chosen = jax.random.permutation(rng, blocks)[partner]
    strong = (owner == chosen) | (owner == (partner + blocks // 2) % blocks)
    return jnp.where(strong, factor * drawn, drawn)


def shard_levels(key, shape, shards, low, high):
    factor_of = 1.0
    for axis_at, shards_of in shards:
        heights = jax.random.uniform(jax.random.fold_in(jax.random.fold_in(key, 6), axis_at), (shards_of,), jnp.float32, low / len(shards), high / len(shards))
        factor_of = factor_of * jnp.repeat(jnp.exp(heights), shape[axis_at] // shards_of).reshape((-1,) + (1,) * (len(shape) - 1 - axis_at))
    return factor_of


def scatter_about(own_key, extent, scale, limit, cuts=(), kind=jnp.bfloat16):
    entries = scale * jax.random.normal(own_key, extent, jnp.float32)
    if cuts:
        entries = entries * shard_levels(own_key, extent, cuts, -0.22, 0.18)
    return jnp.clip(entries, -limit, limit).astype(kind)


def heavy_noise(key, dims, width, most, shards, heavy, kind=jnp.bfloat16):
    entries = width * jax.random.normal(key, dims, jnp.float32)
    if shards:
        entries = entries * shard_levels(key, dims, shards, -0.22, 0.18)
    return jnp.clip(raised(entries, jax.random.fold_in(key, 3), *heavy), -most, most).astype(kind)


def setup_inputs(seed: int = 0) -> dict:
    arg_keys = jax.random.split(jax.random.key(seed), 10)
    return {
        "queries": draw_queries(jax.random.fold_in(arg_keys[9], 71), 0),
        "keys": draw_keys(jax.random.fold_in(arg_keys[9], 71), 0),
        "values": scatter_about(arg_keys[2], (BATCH, SEQLEN, KV_HEADS * HEAD_DIM), 1.0, 4.0, ((0, 2), (1, 8), (2, 2))),
        "query_tangent": scatter_about(arg_keys[3], (BATCH, SEQLEN, HEADS * HEAD_DIM), 1.0, 4.0, ((0, 2), (1, 8), (2, 2))),
        "key_tangent": scatter_about(arg_keys[4], (BATCH, SEQLEN, KV_HEADS * HEAD_DIM), 1.0, 4.0, ((0, 2), (1, 8), (2, 2))),
        "value_tangent": scatter_about(arg_keys[5], (BATCH, SEQLEN, KV_HEADS * HEAD_DIM), 1.0, 4.0, ((0, 2), (1, 8), (2, 2))),
        "lengths": draw_lengths(jax.random.fold_in(arg_keys[9], 71), 0),
        "out_weight": scatter_about(arg_keys[7], (HEADS * HEAD_DIM, D), (HEADS * HEAD_DIM) ** -0.5, 0.125, ((0, 2),)),
        "cotangent": heavy_noise(arg_keys[8], (BATCH, SEQLEN, D), (BATCH * SEQLEN) ** -0.5, 0.1875, ((0, 2), (1, 8)), (1, 2, 8, 2.0)),
    }


def doc_numbers(lengths_row, count):
    ends = jnp.cumsum(lengths_row)
    positions = jnp.arange(count, dtype=jnp.int32)
    return jnp.sum((ends[None, :] <= positions[:, None]).astype(jnp.int32), axis=1)


def reference(queries, keys, values, query_tangent, key_tangent, value_tangent, lengths, out_weight, cotangent):
    group_ratio = HEADS // KV_HEADS
    score_scale = HEAD_DIM ** -0.5
    positions = jnp.arange(SEQLEN, dtype=jnp.int32)

    def split_query(array):
        return array.astype(jnp.float32).reshape(SEQLEN, KV_HEADS, group_ratio, HEAD_DIM).transpose(1, 2, 0, 3)

    def split_key(array):
        return array.astype(jnp.float32).reshape(SEQLEN, KV_HEADS, HEAD_DIM).transpose(1, 0, 2)

    def one_sequence(operands):
        query_seq, key_seq, value_seq, dquery_seq, dkey_seq, dvalue_seq, doc_lens = operands
        docs = doc_numbers(doc_lens, SEQLEN)
        allowed = (docs[:, None] == docs[None, :]) & (positions[None, :] <= positions[:, None])

        def one_group(group_ops):
            query_grp, dquery_grp, key_grp, value_grp, dkey_grp, dvalue_grp = group_ops
            scores = jnp.einsum('rtd,sd->rts', query_grp, key_grp) * score_scale
            tangent = (jnp.einsum('rtd,sd->rts', dquery_grp, key_grp) + jnp.einsum('rtd,sd->rts', query_grp, dkey_grp)) * score_scale
            scores = jnp.where(allowed[None], scores, -1e30)
            highest = jnp.max(scores, axis=-1, keepdims=True)
            weight = jnp.where(allowed[None], jnp.exp(scores - highest), 0.0)
            weighted_tangent = weight * tangent
            total = jnp.sum(weight, axis=-1)
            cross = jnp.sum(weighted_tangent, axis=-1)
            lower_bound = lax.optimization_barrier(weight.astype(jnp.bfloat16)).astype(jnp.float32)
            lower_bound_tangent = lax.optimization_barrier(weighted_tangent.astype(jnp.bfloat16)).astype(jnp.float32)
            running_total = jnp.einsum('rts,sd->rtd', lower_bound, value_grp)
            accum_tangent = jnp.einsum('rts,sd->rtd', lower_bound_tangent, value_grp) + jnp.einsum('rts,sd->rtd', lower_bound, dvalue_grp)
            output = running_total / total[..., None]
            return accum_tangent / total[..., None] - (cross / total)[..., None] * output

        result = lax.map(one_group, (split_query(query_seq), split_query(dquery_seq), split_key(key_seq),
                                     split_key(value_seq), split_key(dkey_seq), split_key(dvalue_seq)))
        return result.transpose(2, 0, 1, 3).reshape(SEQLEN, HEADS * HEAD_DIM).astype(jnp.bfloat16)

    douts = lax.map(one_sequence, (queries, keys, values, query_tangent, key_tangent, value_tangent, lengths))
    flat = douts.reshape(BATCH * SEQLEN, HEADS * HEAD_DIM)
    layer_tangent = jnp.dot(flat, out_weight, preferred_element_type=jnp.float32).astype(jnp.bfloat16)
    layer_tangent = layer_tangent.reshape(BATCH, SEQLEN, D)
    weight_hvp = lax.dot_general(cotangent.reshape(BATCH * SEQLEN, D), flat, (((0,), (0,)), ((), ())),
                                 preferred_element_type=jnp.float32)
    return layer_tangent, weight_hvp
```

```python
import functools

import jax
import jax.numpy as jnp
from jax import lax
from jax.experimental import pallas as pl
from jax.experimental.pallas import tpu as pltpu
from jax.sharding import PartitionSpec as P

HEADS = 16
KV_HEADS = 4
HEAD_DIM = 128
DOC_SHARDS = 2


BF16 = jnp.bfloat16
F32 = jnp.float32


def nt_dot(a, b):
    return lax.dot_general(a, b, (((1,), (1,)), ((), ())), preferred_element_type=F32)


def nn_dot(a, b):
    return lax.dot_general(a, b, (((1,), (0,)), ((), ())), preferred_element_type=F32)


def vmem(count):
    return [pl.BlockSpec(memory_space=pltpu.VMEM) for _ in range(count)]


def pack_kernel(k_ref, v_ref, dk_ref, dv_ref, *outs):
    for g, out in enumerate(outs):
        cols = slice(g * HEAD_DIM, (g + 1) * HEAD_DIM)
        out[0] = k_ref[:, cols]
        out[1] = v_ref[:, cols]
        out[2] = dk_ref[:, cols]
        out[3] = dv_ref[:, cols]


def attend_kernel(lengths_ref, q_ref, dq_ref, *refs):
    blocks, out_ref = refs[:-1], refs[-1]
    tok = q_ref.shape[0]
    ratio = q_ref.shape[1] // HEAD_DIM
    scale = HEAD_DIM ** (-0.5)
    shard = lax.axis_index("seq")
    qpos = shard * tok + lax.broadcasted_iota(jnp.int32, (tok, tok), 0)
    lane = lax.broadcasted_iota(jnp.int32, (tok, tok), 1)
    begin = jnp.zeros((tok, tok), jnp.int32)
    end = jnp.int32(0)
    for i in range(lengths_ref.shape[1]):
        end = end + lengths_ref[0, i]
        begin = jnp.where(qpos >= end, jnp.maximum(begin, end), begin)
    biases = []
    for hop in range(len(blocks)):
        kpos = (shard - hop) * tok + lane
        allowed = (kpos >= begin) & (kpos <= qpos)
        biases.append(jnp.where(allowed, 0.0, -1e30).astype(F32))
    bias = jnp.concatenate(biases, axis=1)
    keys = jnp.concatenate([b[0] for b in blocks], axis=0)
    values = jnp.concatenate([b[1] for b in blocks], axis=0)
    dkeys = jnp.concatenate([b[2] for b in blocks], axis=0)
    dvalues = jnp.concatenate([b[3] for b in blocks], axis=0)
    both_keys = jnp.concatenate([keys, dkeys], axis=1)
    both_values = jnp.concatenate([values, dvalues], axis=0)
    for r in range(ratio):
        cols = slice(r * HEAD_DIM, (r + 1) * HEAD_DIM)
        q, dq = q_ref[:, cols], dq_ref[:, cols]
        scores = nt_dot(q, keys) * scale + bias
        tangent = nt_dot(jnp.concatenate([dq, q], axis=1), both_keys) * scale
        weight = jnp.exp(scores - jnp.max(scores, axis=1, keepdims=True))
        weighted = weight * tangent
        total = jnp.sum(weight, axis=1, keepdims=True)
        cross = jnp.sum(weighted, axis=1, keepdims=True)
        low = weight.astype(BF16)
        accum = nn_dot(low, values)
        accum_tangent = nn_dot(jnp.concatenate([weighted.astype(BF16), low], axis=1), both_values)
        out_ref[:, cols] = (accum_tangent / total - (cross / total) * (accum / total)).astype(BF16)


def turn_kernel(inner, cot_ref, *outs):
    places = len(outs)
    outer = places // inner
    share = outs[0].shape[0]
    parts = lax.axis_size("head")
    shard, part = lax.axis_index("seq"), lax.axis_index("head")
    z, x = shard // inner, shard % inner
    for k in range(outer):
        for e in range(inner):
            dest = ((z + k) % outer) * inner + (x + e) % inner
            first = (dest * parts + part) * share
            block = cot_ref[:, pl.ds(pl.multiple_of(first, 128), share)]
            outs[k * inner + e][...] = block.T


def join_kernel(*refs):
    out_ref = refs[-1]
    for i, piece in enumerate(refs[:-1]):
        tok = piece.shape[1]
        out_ref[:, i * tok:(i + 1) * tok] = piece[...]


def project_kernel(offset, *refs):
    douts, weight_ref = refs[:-2], refs[-2]
    out_ref = refs[-1]
    width = douts[0].shape[1]
    out = nn_dot(douts[0][...], weight_ref[:width])
    for i in range(1, len(douts)):
        out = out + nn_dot(douts[i][...], weight_ref[i * width:(i + 1) * width])
    out_ref[...] = out.astype(out_ref.dtype)


def project_add_kernel(count, *refs):
    douts, weight_ref, others, out_ref = refs[:count], refs[count], refs[count + 1:-1], refs[-1]
    width = douts[0].shape[1]
    out = nn_dot(douts[0][...], weight_ref[:width])
    for i in range(1, count):
        out = out + nn_dot(douts[i][...], weight_ref[i * width:(i + 1) * width])
    for other in others:
        out = out + other[...].astype(F32)
    out_ref[...] = out.astype(out_ref.dtype)


def product_kernel(halves, shifts, *refs):
    cots, pieces = refs[:halves], refs[halves:len(refs) - len(shifts) - 1]
    outs, all_ref = refs[len(refs) - len(shifts) - 1:-1], refs[-1]
    count = lax.axis_size("dp")
    own, part = lax.axis_index("dp"), lax.axis_index("head")
    share = cots[0].shape[0]
    for i in range(halves):
        at = pl.multiple_of(((part + i) % halves) * share, 16)
        all_ref[pl.ds(at, share), :] = cots[i][...]
    dout = jnp.concatenate([piece[...] for piece in pieces], axis=0)
    rows = outs[0].shape[0]
    for shift, out in zip(shifts, outs):
        first = pl.multiple_of(((own + shift) % count) * rows, 16)
        out[...] = nn_dot(all_ref[pl.ds(first, rows), :], dout).astype(out.dtype)


def finish_kernel(groups, *refs):
    out_ref = refs[-1]
    each = (len(refs) - 1) // groups
    for g in range(groups):
        mine = refs[g * each:(g + 1) * each]
        width = mine[0].shape[1]
        out = mine[0][...]
        for other in mine[1:]:
            out = out + other[...].astype(F32)
        out_ref[:, g * width:(g + 1) * width] = out


def on_device(inner, queries, keys, values, query_tangent, key_tangent, value_tangent, lengths, out_weight, cotangent):
    tok = queries.shape[1]
    seq_count, dp_count, head_count = (lax.axis_size(a) for a in ("seq", "dp", "head"))
    outer = seq_count // inner
    groups = keys.shape[2] // HEAD_DIM
    group_width = queries.shape[2] // groups
    model = out_weight.shape[1]

    def along(axis, count, shift):
        return functools.partial(lax.ppermute, axis_name=axis, perm=[(i, (i + shift) % count) for i in range(count)])

    def to_place(k, e):
        perm = []
        for i in range(seq_count):
            z, x = divmod(i, inner)
            perm.append((i, ((z + k) % outer) * inner + (x + e) % inner))
        return functools.partial(lax.ppermute, axis_name="seq", perm=perm)

    def behind(block, hop):
        return lax.ppermute(block, "seq", [(i, i + hop) for i in range(seq_count - hop)])

    packed = pl.pallas_call(
        pack_kernel,
        out_shape=[jax.ShapeDtypeStruct((4, tok, HEAD_DIM), BF16)] * groups,
        in_specs=vmem(4),
        out_specs=vmem(groups),
        name="pack",
    )(keys[0], values[0], key_tangent[0], value_tangent[0])
    halos = [[packed[g]] + [behind(packed[g], hop) for hop in range(1, DOC_SHARDS + 1)] for g in range(groups)]

    share = model // (seq_count * head_count)
    turned = pl.pallas_call(
        functools.partial(turn_kernel, inner),
        out_shape=[jax.ShapeDtypeStruct((share, tok), BF16)] * seq_count,
        in_specs=vmem(1),
        out_specs=vmem(seq_count),
        name="turn",
    )(cotangent[0])

    douts = []
    for g in range(groups):
        attend = pl.pallas_call(
            attend_kernel,
            out_shape=jax.ShapeDtypeStruct((tok, group_width), BF16),
            grid=(1,),
            in_specs=[
                pl.BlockSpec(memory_space=pltpu.SMEM),
                pl.BlockSpec((tok, group_width), lambda i, g=g: (0, g)),
                pl.BlockSpec((tok, group_width), lambda i, g=g: (0, g)),
            ]
            + [pl.BlockSpec((4, tok, HEAD_DIM), lambda i: (0, 0, 0))] * (DOC_SHARDS + 1),
            out_specs=pl.BlockSpec((tok, group_width), lambda i: (0, 0)),
            name=f"attend_{g}",
        )
        douts.append(attend(lengths, queries[0], query_tangent[0], *halos[g]))

    pieces = []
    for g in range(groups):
        column = [douts[g]] + [to_place(k, 0)(douts[g]) for k in range(1, outer)]
        pieces.append([to_place(0, e)(c) if e else c for c in column for e in range(inner)])

    cot_pieces = [
        to_place(*divmod(i, inner))(turned[i]) if i else turned[i] for i in range(seq_count)
    ]
    cot_own = pl.pallas_call(
        join_kernel,
        out_shape=jax.ShapeDtypeStruct((share, tok * seq_count), BF16),
        in_specs=vmem(seq_count),
        out_specs=vmem(1)[0],
        name="join",
    )(*cot_pieces)
    cots = [cot_own] + [along("head", head_count, -s)(cot_own) for s in range(1, head_count)]

    out_cols = model // head_count
    step = 512 if out_cols % 512 == 0 else out_cols
    blocks = out_cols // step

    def project(shift, others):
        part = (lax.axis_index("head") + shift) % head_count
        kernel = functools.partial(project_add_kernel, groups)
        grid_spec = pltpu.PrefetchScalarGridSpec(
            num_scalar_prefetch=1,
            grid=(blocks,),
            in_specs=[pl.BlockSpec((tok, group_width), lambda i, p: (0, 0))] * groups
            + [pl.BlockSpec((group_width * groups, step), lambda i, p: (0, p[0] * blocks + i))]
            + [pl.BlockSpec((tok, step), lambda i, p: (0, i))] * len(others),
            out_specs=pl.BlockSpec((tok, step), lambda i, p: (0, i)),
        )
        return pl.pallas_call(
            lambda p_ref, *refs: kernel(*refs),
            out_shape=jax.ShapeDtypeStruct((tok, out_cols), BF16),
            grid_spec=grid_spec,
            name=f"project_{shift}",
        )(part.reshape(1).astype(jnp.int32), *douts, out_weight, *others)

    others = [along("head", head_count, s)(project(s, [])) for s in range(1, head_count)]
    layer_tangent = project(0, others)

    rows = model // (seq_count * dp_count)

    def product(g, shifts, dtype, name):
        return pl.pallas_call(
            functools.partial(product_kernel, head_count, shifts),
            out_shape=[jax.ShapeDtypeStruct((rows, group_width), dtype)] * len(shifts),
            in_specs=vmem(head_count + seq_count),
            out_specs=vmem(len(shifts)),
            scratch_shapes=[pltpu.VMEM((share * head_count, tok * seq_count), BF16)],
            name=name,
        )(*cots, *pieces[g])

    parts = []
    shifts = tuple(range(1, dp_count))
    for g in range(groups):
        sent = product(g, shifts, BF16, f"send_{g}")
        got = [along("dp", dp_count, s)(block) for s, block in zip(shifts, sent)]
        kept = product(g, (0,), F32, f"keep_{g}")
        parts += [*kept, *got]
    weight_hvp = pl.pallas_call(
        functools.partial(finish_kernel, groups),
        out_shape=jax.ShapeDtypeStruct((rows, group_width * groups), F32),
        in_specs=vmem(len(parts)),
        out_specs=vmem(1)[0],
        name="finish",
    )(*parts)
    return (layer_tangent[None], weight_hvp)


def solution(mesh):
    inner = 2 if mesh.shape["seq"] % 2 == 0 else 1
    placed = (
        P("dp", "seq", "head"),
        P("dp", "seq", "head"),
        P("dp", "seq", "head"),
        P("dp", "seq", "head"),
        P("dp", "seq", "head"),
        P("dp", "seq", "head"),
        P("dp", None),
        P("head", None),
        P("dp", "seq", None),
    )
    return jax.shard_map(
        functools.partial(on_device, inner),
        mesh=mesh,
        in_specs=placed,
        out_specs=(P("dp", "seq", "head"), P(("seq", "dp"), "head")),
        check_vma=False,
    )
```

```python
import functools

import jax
import jax.numpy as jnp
from jax import lax
from jax.experimental import pallas as pl
from jax.experimental.pallas import tpu as pltpu
from jax.sharding import PartitionSpec as P

HEAD_DIM = 128
DOC_SHARDS = 2
INNER = 2
CHUNKS = 2


BF16 = jnp.bfloat16
F32 = jnp.float32
VMEM = pltpu.VMEM


def nt_dot(a, b):
    return lax.dot_general(a, b, (((1,), (1,)), ((), ())), preferred_element_type=F32)


def nn_dot(a, b):
    return lax.dot_general(a, b, (((1,), (0,)), ((), ())), preferred_element_type=F32)


def specs(count):
    return [pl.BlockSpec(memory_space=VMEM) for _ in range(count)]


def near(array):
    return pltpu.with_memory_space_constraint(array, VMEM)


def pack_kernel(k_ref, v_ref, dk_ref, dv_ref, *outs):
    x = lax.axis_index("seq") % INNER
    for i, out in enumerate(outs):
        group = (x + 1 + i) % len(outs)
        cols = pl.ds(pl.multiple_of(group * HEAD_DIM, HEAD_DIM), HEAD_DIM)
        for j, ref in enumerate((k_ref, v_ref, dk_ref, dv_ref)):
            out[j] = ref[:, cols]


def attend_kernel(order, groups, lengths_ref, q_ref, dq_ref, *refs):
    blocks, out_ref = refs[:-1], refs[-1]
    tok, width = out_ref.shape
    scale = HEAD_DIM ** (-0.5)
    shard = lax.axis_index("seq")
    group = (shard % INNER + 1 + order) % groups
    qpos = shard * tok + lax.broadcasted_iota(jnp.int32, (tok, tok), 0)
    lane = lax.broadcasted_iota(jnp.int32, (tok, tok), 1)
    begin = jnp.zeros((tok, tok), jnp.int32)
    end = jnp.int32(0)
    for i in range(lengths_ref.shape[1]):
        end = end + lengths_ref[0, i]
        begin = jnp.where(qpos >= end, jnp.maximum(begin, end), begin)
    biases = []
    for hop in range(len(blocks)):
        kpos = (shard - hop) * tok + lane
        allowed = (kpos >= begin) & (kpos <= qpos)
        biases.append(jnp.where(allowed, 0.0, -1e30).astype(F32))
    bias = jnp.concatenate(biases, axis=1)
    keys = jnp.concatenate([b[0] for b in blocks], axis=0)
    values = jnp.concatenate([b[1] for b in blocks], axis=0)
    dkeys = jnp.concatenate([b[2] for b in blocks], axis=0)
    dvalues = jnp.concatenate([b[3] for b in blocks], axis=0)
    both_keys = jnp.concatenate([keys, dkeys], axis=1)
    both_values = jnp.concatenate([values, dvalues], axis=0)
    for r in range(width // HEAD_DIM):
        cols = pl.ds(pl.multiple_of(group * width + r * HEAD_DIM, HEAD_DIM), HEAD_DIM)
        q, dq = q_ref[:, cols], dq_ref[:, cols]
        scores = nt_dot(q, keys) * scale + bias
        tangent = nt_dot(jnp.concatenate([dq, q], axis=1), both_keys) * scale
        weight = jnp.exp(scores - jnp.max(scores, axis=1, keepdims=True))
        weighted = weight * tangent
        total = jnp.sum(weight, axis=1, keepdims=True)
        cross = jnp.sum(weighted, axis=1, keepdims=True)
        low = weight.astype(BF16)
        accum = nn_dot(low, values)
        accum_tangent = nn_dot(jnp.concatenate([weighted.astype(BF16), low], axis=1), both_values)
        out = accum_tangent / total - (cross / total) * (accum / total)
        out_ref[:, r * HEAD_DIM:(r + 1) * HEAD_DIM] = out.astype(BF16)


def turn_kernel(cot_ref, *outs):
    outer = len(outs)
    share = outs[0].shape[0]
    parts = lax.axis_size("head")
    z, part = lax.axis_index("seq") // INNER, lax.axis_index("head")
    for k in range(outer):
        first = (((z + k) % outer) * parts + part) * share
        outs[k][...] = cot_ref[:, pl.ds(pl.multiple_of(first, 128), share)].T


def join_kernel(*refs):
    out_ref = refs[-1]
    for i, piece in enumerate(refs[:-1]):
        tok = piece.shape[1]
        out_ref[:, i * tok:(i + 1) * tok] = piece[...]


def merge_kernel(own_ref, got_ref, *outs):
    tok = own_ref.shape[0]
    for j, out in enumerate(outs):
        width = out.shape[1]
        out[:tok] = own_ref[:, j * width:(j + 1) * width]
        out[tok:] = got_ref[:, j * width:(j + 1) * width]


def project_kernel(p_ref, first_ref, last_ref, weight_ref, *refs):
    others, out_ref = refs[:-1], refs[-1]
    width = first_ref.shape[1]
    groups = weight_ref.shape[0] // width
    x = lax.axis_index("seq") % INNER
    out = None
    for i, dout in enumerate((first_ref, last_ref)):
        at = pl.multiple_of(((x + 1 + i) % groups) * width, width)
        part = nn_dot(dout[...], weight_ref[pl.ds(at, width), :])
        out = part if out is None else out + part
    for other in others:
        out = out + other[...].astype(F32)
    out_ref[...] = out.astype(out_ref.dtype)


def product_kernel(shifts, *refs):
    cots = refs[:2 * INNER]
    pieces, outs = refs[2 * INNER:-len(shifts)], refs[-len(shifts):]
    count = lax.axis_size("dp")
    x, own, part = lax.axis_index("seq") % INNER, lax.axis_index("dp"), lax.axis_index("head")
    tok = pieces[0].shape[0] // INNER
    douts = [jnp.concatenate([p[e * tok:(e + 1) * tok] for p in pieces], axis=0) for e in range(INNER)]
    rows = outs[0].shape[0]
    for (dx, dy), out in zip(shifts, outs):
        half = (x + dx) % INNER
        at = pl.ds(pl.multiple_of(((own + dy) % count) * rows, 16), rows)

        def fill(halves, out=out, at=at):
            total = nn_dot(halves[0][at, :], douts[0])
            for e in range(1, INNER):
                total = total + nn_dot(halves[e][at, :], douts[e])
            out[...] = total.astype(out.dtype)

        pl.when(half == part)(functools.partial(fill, cots[:INNER]))
        pl.when(half != part)(functools.partial(fill, cots[INNER:]))


def finish_kernel(*refs):
    out_ref = refs[-1]
    each = (len(refs) - 1) // CHUNKS
    x = lax.axis_index("seq") % INNER
    span = out_ref.shape[1] // INNER
    for j in range(CHUNKS):
        mine = refs[j * each:(j + 1) * each]
        side = each // INNER
        for dx in range(INNER):
            out = mine[dx * side][...].astype(F32)
            for other in mine[dx * side + 1:(dx + 1) * side]:
                out = out + other[...].astype(F32)
            width = out.shape[1]
            group = (x - dx) % INNER
            at = pl.multiple_of(group * span + j * width, 128)
            out_ref[:, pl.ds(at, width)] = out


def on_device(queries, keys, values, query_tangent, key_tangent, value_tangent, lengths, out_weight, cotangent):
    tok = queries.shape[1]
    seq_count, dp_count, head_count = (lax.axis_size(a) for a in ("seq", "dp", "head"))
    outer = seq_count // INNER
    groups = keys.shape[2] // HEAD_DIM
    width = queries.shape[2] // groups
    model = out_weight.shape[1]
    assert groups == INNER and head_count == INNER

    def call(kernel, shapes, *args, far=0):
        args = args[:far] + tuple(near(a) for a in args[far:])
        return pl.pallas_call(
            kernel,
            out_shape=[s if isinstance(s, jax.ShapeDtypeStruct) else VMEM(*s) for s in shapes],
            in_specs=specs(len(args)),
            out_specs=specs(len(shapes)),
        )(*args)

    def outward(block, k):
        return lax.ppermute(block, "seq", [(i, (i + k * INNER) % seq_count) for i in range(seq_count)])

    def across(block):
        return lax.ppermute(block, "seq", [(i, i // INNER * INNER + (i + 1) % INNER) for i in range(seq_count)])

    def aside(block, s):
        return lax.ppermute(block, "head", [(i, (i + s) % head_count) for i in range(head_count)])

    def to_owner(block, dx, dy):
        perm = []
        for i in range(seq_count):
            for d in range(dp_count):
                to = i // INNER * INNER + (i + dx) % INNER
                perm.append((i * dp_count + d, to * dp_count + (d + dy) % dp_count))
        return lax.ppermute(block, ("seq", "dp"), perm)

    packed = call(pack_kernel, [((4, tok, HEAD_DIM), BF16)] * groups, keys[0], values[0], key_tangent[0], value_tangent[0], far=4)
    halos = []
    for i in range(groups):
        halo = [packed[i]]
        for hop in range(1, DOC_SHARDS + 1):
            perm = [(s, s + hop) for s in range(seq_count - hop)]
            halo.append(lax.ppermute(packed[(i + hop) % groups], "seq", perm))
        halos.append(halo)

    share = model // (outer * head_count)
    turned = call(turn_kernel, [((share, tok), BF16)] * outer, cotangent[0], far=1)
    arrived = [turned[0]] + [outward(turned[k], k) for k in range(1, outer)]
    (cot_own,) = call(join_kernel, [((share, tok * outer), BF16)], *arrived)
    cot_next = across(cot_own)
    cots = [cot_own, cot_next, aside(cot_own, 1), aside(cot_next, 1)]

    douts = []
    for i in range(groups):
        douts.append(
            pl.pallas_call(
                functools.partial(attend_kernel, i, groups),
                out_shape=VMEM((tok, width), BF16),
                in_specs=[pl.BlockSpec(memory_space=pltpu.SMEM)] + specs(2 + len(halos[i])),
                out_specs=specs(1)[0],
            )(lengths, queries[0], query_tangent[0], *(near(b) for b in halos[i]))
        )
    got = across(douts[0])
    merged = call(merge_kernel, [((INNER * tok, width // CHUNKS), BF16)] * CHUNKS, douts[1], got)
    far_first = sorted(range(1, outer), key=lambda k: abs(k - outer / 2))
    pieces = []
    for j in range(CHUNKS):
        came = {k: outward(merged[j], k) for k in far_first}
        pieces.append([merged[j]] + [came[k] for k in range(1, outer)])

    out_cols = model // head_count
    step = 512 if out_cols % 512 == 0 else out_cols
    blocks = out_cols // step

    def project(shift, others):
        part = ((lax.axis_index("head") + shift) % head_count).reshape(1).astype(jnp.int32)
        grid_spec = pltpu.PrefetchScalarGridSpec(
            num_scalar_prefetch=1,
            grid=(blocks,),
            in_specs=specs(groups)
            + [pl.BlockSpec((width * groups, step), lambda i, p: (0, p[0] * blocks + i))]
            + [pl.BlockSpec((tok, step), lambda i, p: (0, i))] * len(others),
            out_specs=pl.BlockSpec((tok, step), lambda i, p: (0, i)),
        )
        return pl.pallas_call(
            project_kernel, out_shape=jax.ShapeDtypeStruct((tok, out_cols), BF16), grid_spec=grid_spec
        )(part, *(near(d) for d in douts), out_weight, *others)

    others = [aside(project(1, []), 1)]
    layer_tangent = project(0, others)

    rows = model // (seq_count * dp_count)
    order = [(dx, dy) for dx in reversed(range(INNER)) for dy in reversed(range(dp_count)) if dx or dy]
    parts = []
    for j in range(CHUNKS):
        shape = ((rows, width // CHUNKS), BF16)
        sent = call(functools.partial(product_kernel, order), [shape] * len(order), *cots, *pieces[j])
        came = {at: to_owner(block, *at) for at, block in zip(order, sent)}
        (mine,) = call(functools.partial(product_kernel, [(0, 0)]), [((rows, width // CHUNKS), F32)], *cots, *pieces[j])
        came[(0, 0)] = mine
        parts += [came[(dx, dy)] for dx in range(INNER) for dy in range(dp_count)]
    (weight_hvp,) = call(finish_kernel, [jax.ShapeDtypeStruct((rows, width * groups), F32)], *parts)
    return (layer_tangent[None], weight_hvp)


def solution(mesh):
    placed = (
        P("dp", "seq", "head"),
        P("dp", "seq", "head"),
        P("dp", "seq", "head"),
        P("dp", "seq", "head"),
        P("dp", "seq", "head"),
        P("dp", "seq", "head"),
        P("dp", None),
        P("head", None),
        P("dp", "seq", None),
    )

    return jax.shard_map(
        on_device,
        mesh=mesh,
        in_specs=placed,
        out_specs=(P("dp", "seq", "head"), P(("seq", "dp"), "head")),
        check_vma=False,
    )
```

```python
import functools

import jax
import jax.numpy as jnp
from jax import lax
from jax.experimental import pallas as pl
from jax.experimental.pallas import tpu as pltpu
from jax.sharding import PartitionSpec as P

HEAD_DIM = 128
DOC_SHARDS = 2
INNER = 2
CHUNKS = 2


BF16 = jnp.bfloat16
F32 = jnp.float32
VMEM = pltpu.VMEM
PARAMS = pltpu.CompilerParams(vmem_limit_bytes=12 * 1024 * 1024)


def nt_dot(a, b):
    return lax.dot_general(a, b, (((1,), (1,)), ((), ())), preferred_element_type=F32)


def nn_dot(a, b):
    return lax.dot_general(a, b, (((1,), (0,)), ((), ())), preferred_element_type=F32)


def specs(count):
    return [pl.BlockSpec(memory_space=VMEM) for _ in range(count)]


def near(array):
    return pltpu.with_memory_space_constraint(array, VMEM)


def far(array):
    return pltpu.with_memory_space_constraint(array, pltpu.HBM)


def pack_kernel(k_ref, v_ref, dk_ref, dv_ref, *outs):
    for i, out in enumerate(outs):
        cols = slice(i * HEAD_DIM, (i + 1) * HEAD_DIM)
        for j, ref in enumerate((k_ref, v_ref, dk_ref, dv_ref)):
            out[j] = ref[:, cols]


def pick_kernel(own_ref, back_ref, out_ref):
    x = lax.axis_index("seq") % INNER

    @pl.when(x == 0)
    def _():
        out_ref[...] = own_ref[...]

    @pl.when(x != 0)
    def _():
        out_ref[...] = back_ref[...]


def attend_kernel(order, groups, lengths_ref, q_ref, dq_ref, *refs):
    owns, backs, near_ref, out_ref = refs[:groups], refs[groups:2 * groups], refs[-2], refs[-1]
    tok, width = out_ref.shape
    scale = HEAD_DIM ** (-0.5)
    shard = lax.axis_index("seq")
    group = (shard % INNER + 1 + order) % groups
    qpos = shard * tok + lax.broadcasted_iota(jnp.int32, (tok, tok), 0)
    lane = lax.broadcasted_iota(jnp.int32, (tok, tok), 1)
    begin = jnp.zeros((tok, tok), jnp.int32)
    end = jnp.int32(0)
    for i in range(lengths_ref.shape[1]):
        end = end + lengths_ref[0, i]
        begin = jnp.where(qpos >= end, jnp.maximum(begin, end), begin)
    biases = []
    for hop in range(DOC_SHARDS + 1):
        kpos = (shard - hop) * tok + lane
        allowed = (kpos >= begin) & (kpos <= qpos)
        biases.append(jnp.where(allowed, 0.0, -1e30).astype(F32))
    bias = jnp.concatenate(biases, axis=1)
    own = jnp.where(group == 0, owns[0][...], owns[1][...])
    back = jnp.where(group == 0, backs[0][...], backs[1][...])
    blocks = (own, near_ref, back)
    keys = jnp.concatenate([b[0] for b in blocks], axis=0)
    values = jnp.concatenate([b[1] for b in blocks], axis=0)
    dkeys = jnp.concatenate([b[2] for b in blocks], axis=0)
    dvalues = jnp.concatenate([b[3] for b in blocks], axis=0)
    both_keys = jnp.concatenate([keys, dkeys], axis=1)
    both_values = jnp.concatenate([values, dvalues], axis=0)
    for r in range(width // HEAD_DIM):
        cols = pl.ds(pl.multiple_of(group * width + r * HEAD_DIM, HEAD_DIM), HEAD_DIM)
        q, dq = q_ref[:, cols], dq_ref[:, cols]
        scores = nt_dot(q, keys) * scale + bias
        tangent = nt_dot(jnp.concatenate([dq, q], axis=1), both_keys) * scale
        weight = jnp.exp(scores - jnp.max(scores, axis=1, keepdims=True))
        weighted = weight * tangent
        total = jnp.sum(weight, axis=1, keepdims=True)
        cross = jnp.sum(weighted, axis=1, keepdims=True)
        low = weight.astype(BF16)
        accum = nn_dot(low, values)
        accum_tangent = nn_dot(jnp.concatenate([weighted.astype(BF16), low], axis=1), both_values)
        out = accum_tangent / total - (cross / total) * (accum / total)
        out_ref[:, r * HEAD_DIM:(r + 1) * HEAD_DIM] = out.astype(BF16)


def turn_kernel(cot_ref, q_ref, dq_ref, *outs):
    outs, (near_q, near_dq, sems) = outs[:-3], outs[-3:]
    fetches = [pltpu.make_async_copy(q_ref, near_q, sems.at[0]), pltpu.make_async_copy(dq_ref, near_dq, sems.at[1])]
    for fetch in fetches:
        fetch.start()
    outer = len(outs)
    share = outs[0].shape[0]
    parts = lax.axis_size("head")
    z, part = lax.axis_index("seq") // INNER, lax.axis_index("head")
    for k in range(outer):
        first = ((z ^ k) * parts + part) * share
        outs[k][...] = cot_ref[:, pl.ds(pl.multiple_of(first, 128), share)].T
    for fetch in fetches:
        fetch.wait()


def join_kernel(*refs):
    out_ref = refs[-1]
    for i, piece in enumerate(refs[:-1]):
        tok = piece.shape[1]
        out_ref[:, i * tok:(i + 1) * tok] = piece[...]


def merge_kernel(own_ref, got_ref, *outs):
    tok = own_ref.shape[0]
    for j, out in enumerate(outs):
        width = out.shape[1]
        out[:tok] = own_ref[:, j * width:(j + 1) * width]
        out[tok:] = got_ref[:, j * width:(j + 1) * width]


def project_kernel(p_ref, first_ref, last_ref, weight_ref, *refs):
    others, out_ref = refs[:-1], refs[-1]
    width = first_ref.shape[1]
    groups = weight_ref.shape[0] // width
    x = lax.axis_index("seq") % INNER
    out = None
    for i, dout in enumerate((first_ref, last_ref)):
        at = pl.multiple_of(((x + 1 + i) % groups) * width, width)
        part = nn_dot(dout[...], weight_ref[pl.ds(at, width), :])
        out = part if out is None else out + part
    for other in others:
        out = out + other[...].astype(F32)
    out_ref[...] = out.astype(out_ref.dtype)


def product_kernel(shifts, folded, *refs):
    cots = refs[:4 * INNER]
    pieces, outs = refs[4 * INNER:-len(shifts)], refs[-len(shifts):]
    count = lax.axis_size("dp")
    x, own, part = lax.axis_index("seq") % INNER, lax.axis_index("dp"), lax.axis_index("head")
    z = lax.axis_index("seq") // INNER
    blocks = [p[...] for p in pieces]
    if folded:
        edge = (z == 0) | (z == 3)
        blocks = blocks[:3] + [jnp.where(edge, blocks[4], blocks[3])]
    tok = pieces[0].shape[0] // INNER
    half_count = len(blocks) // 2
    douts = []
    for e in range(INNER):
        for i in range(2):
            own_blocks = blocks[i * half_count:(i + 1) * half_count]
            douts.append(jnp.concatenate([b[e * tok:(e + 1) * tok] for b in own_blocks], axis=0))
    rows = outs[0].shape[0]
    for (dx, dy), out in zip(shifts, outs):
        half = (x + dx) % INNER
        at = pl.ds(pl.multiple_of(((own + dy) % count) * rows, 16), rows)

        def fill(halves, out=out, at=at):
            total = nn_dot(halves[0][at, :], douts[0])
            for e in range(1, len(douts)):
                total = total + nn_dot(halves[e][at, :], douts[e])
            out[...] = total.astype(out.dtype)

        pl.when(half == part)(functools.partial(fill, cots[:2 * INNER]))
        pl.when(half != part)(functools.partial(fill, cots[2 * INNER:]))


def finish_kernel(*refs):
    out_ref = refs[-1]
    each = (len(refs) - 1) // CHUNKS
    x = lax.axis_index("seq") % INNER
    span = out_ref.shape[1] // INNER
    for j in range(CHUNKS):
        mine = refs[j * each:(j + 1) * each]
        side = each // INNER
        for dx in range(INNER):
            out = mine[dx * side][...].astype(F32)
            for other in mine[dx * side + 1:(dx + 1) * side]:
                out = out + other[...].astype(F32)
            width = out.shape[1]
            group = (x - dx) % INNER
            at = pl.multiple_of(group * span + j * width, 128)
            out_ref[:, pl.ds(at, width)] = out


def on_device(queries, keys, values, query_tangent, key_tangent, value_tangent, lengths, out_weight, cotangent):
    tok = queries.shape[1]
    seq_count, dp_count, head_count = (lax.axis_size(a) for a in ("seq", "dp", "head"))
    outer = seq_count // INNER
    groups = keys.shape[2] // HEAD_DIM
    width = queries.shape[2] // groups
    model = out_weight.shape[1]
    assert groups == INNER and head_count == INNER

    def call(kernel, shapes, *args, given=0):
        args = args[:given] + tuple(near(a) for a in args[given:])
        return pl.pallas_call(
            kernel,
            out_shape=[s if isinstance(s, jax.ShapeDtypeStruct) else VMEM(*s) for s in shapes],
            in_specs=specs(len(args)),
            out_specs=specs(len(shapes)),
            compiler_params=PARAMS,
        )(*args)

    def outward(block, k):
        return lax.ppermute(block, "seq", [(i, i ^ (k * INNER)) for i in range(seq_count)])

    def across(block):
        return lax.ppermute(block, "seq", [(i, i // INNER * INNER + (i + 1) % INNER) for i in range(seq_count)])

    def aside(block, s):
        return lax.ppermute(block, "head", [(i, (i + s) % head_count) for i in range(head_count)])

    def to_owner(block, dx, dy):
        perm = []
        for i in range(seq_count):
            for d in range(dp_count):
                to = i // INNER * INNER + (i + dx) % INNER
                perm.append((i * dp_count + d, to * dp_count + (d + dy) % dp_count))
        return lax.ppermute(block, ("seq", "dp"), perm)

    packed = call(pack_kernel, [((4, tok, HEAD_DIM), BF16)] * groups, *(far(a[0]) for a in (keys, values, key_tangent, value_tangent)), given=4)
    hop = [(i, i + INNER) for i in range(seq_count - INNER)]
    backs = {g: lax.ppermute(packed[g], "seq", hop) for g in reversed(range(groups))}
    nears = []
    for i in range(groups):
        (picked,) = call(pick_kernel, [((4, tok, HEAD_DIM), BF16)], packed[i], backs[1 - i])
        nears.append(across(picked))

    share = model // (outer * head_count)
    *turned, near_q, near_dq = pl.pallas_call(
        turn_kernel,
        out_shape=[VMEM((share, tok), BF16)] * outer + [VMEM((tok, width * groups), BF16)] * 2,
        in_specs=specs(1) + [pl.BlockSpec(memory_space=pltpu.HBM)] * 2,
        out_specs=specs(outer + 2),
        scratch_shapes=[pltpu.SemaphoreType.DMA((2,))],
        compiler_params=PARAMS,
        name="turn",
    )(far(cotangent[0]), far(queries[0]), far(query_tangent[0]))
    arrived = [turned[0]] + [outward(turned[k], k) for k in range(1, outer)]
    owns, nexts = [], []
    for i in range(2):
        segment = arrived[i * outer // 2:(i + 1) * outer // 2]
        owns += call(join_kernel, [((share, tok * len(segment)), BF16)], *segment)
        nexts.append(across(owns[i]))
    cots = [*owns, *nexts]
    cots += [aside(c, 1) for c in cots]

    douts = []
    for i in range(groups):
        douts.append(
            pl.pallas_call(
                functools.partial(attend_kernel, i, groups),
                out_shape=VMEM((tok, width), BF16),
                in_specs=[pl.BlockSpec(memory_space=pltpu.SMEM)] + specs(3 + 2 * groups),
                out_specs=specs(1)[0],
                compiler_params=PARAMS,
            )(far(lengths), near(near_q), near(near_dq), *(near(b) for b in (*packed, backs[0], backs[1], nears[i])))
        )
    got = across(douts[0])
    merged = call(merge_kernel, [((INNER * tok, width // CHUNKS), BF16)] * CHUNKS, douts[1], got)
    folded = outer == 4
    pieces = []
    for j in range(CHUNKS):
        came = [outward(merged[j], k) for k in range(1, outer - folded)]
        if folded:
            middle = [(z * INNER + x, (z ^ 3) * INNER + x) for z in (1, 2) for x in range(INNER)]
            ends = [(z * INNER + x, (z ^ 1) * INNER + x) for z in (1, 2) for x in range(INNER)]
            came.append(lax.ppermute(merged[j], "seq", middle))
            came.append(lax.ppermute(came[1], "seq", ends))
        pieces.append([merged[j]] + came)

    out_cols = model // head_count
    step = 512 if out_cols % 512 == 0 else out_cols
    blocks = out_cols // step

    def project(shift, others):
        part = ((lax.axis_index("head") + shift) % head_count).reshape(1).astype(jnp.int32)
        grid_spec = pltpu.PrefetchScalarGridSpec(
            num_scalar_prefetch=1,
            grid=(blocks,),
            in_specs=specs(groups)
            + [pl.BlockSpec((width * groups, step), lambda i, p: (0, p[0] * blocks + i))]
            + [pl.BlockSpec((tok, step), lambda i, p: (0, i))] * len(others),
            out_specs=pl.BlockSpec((tok, step), lambda i, p: (0, i)),
        )
        return pl.pallas_call(
            project_kernel,
            out_shape=jax.ShapeDtypeStruct((tok, out_cols), BF16),
            grid_spec=grid_spec,
            compiler_params=PARAMS,
        )(part, *(near(d) for d in douts), far(out_weight), *others)

    others = [aside(project(1, []), 1)]
    layer_tangent = project(0, others)

    rows = model // (seq_count * dp_count)
    order = [(dx, dy) for dx in reversed(range(INNER)) for dy in reversed(range(dp_count)) if dx or dy]
    parts = []
    for j in range(CHUNKS):
        shape = (rows, width // CHUNKS)
        *sent, mine = call(
            functools.partial(product_kernel, order + [(0, 0)], folded),
            [(shape, BF16)] * len(order) + [(shape, F32)],
            *cots,
            *pieces[j],
        )
        came = {at: to_owner(block, *at) for at, block in zip(order, sent)}
        came[(0, 0)] = mine
        parts += [came[(dx, dy)] for dx in range(INNER) for dy in range(dp_count)]
    (weight_hvp,) = call(finish_kernel, [jax.ShapeDtypeStruct((rows, width * groups), F32)], *parts)
    return (layer_tangent[None], weight_hvp)


def solution(mesh):
    placed = (
        P("dp", "seq", "head"),
        P("dp", "seq", "head"),
        P("dp", "seq", "head"),
        P("dp", "seq", "head"),
        P("dp", "seq", "head"),
        P("dp", "seq", "head"),
        P("dp", None),
        P("head", None),
        P("dp", "seq", None),
    )

    return jax.shard_map(
        on_device,
        mesh=mesh,
        in_specs=placed,
        out_specs=(P("dp", "seq", "head"), P(("seq", "dp"), "head")),
        check_vma=False,
    )
```

```python
import functools

import jax
import jax.numpy as jnp
from jax import lax
from jax.experimental import pallas as pl
from jax.experimental.pallas import tpu as pltpu
from jax.sharding import PartitionSpec as P

HEAD_DIM = 128
DOC_SHARDS = 2
INNER = 2
CHUNKS = 2


BF16 = jnp.bfloat16
F32 = jnp.float32
VMEM = pltpu.VMEM
PARAMS = pltpu.CompilerParams(vmem_limit_bytes=12 * 1024 * 1024)


def nt_dot(a, b):
    return lax.dot_general(a, b, (((1,), (1,)), ((), ())), preferred_element_type=F32)


def nn_dot(a, b):
    return lax.dot_general(a, b, (((1,), (0,)), ((), ())), preferred_element_type=F32)


def specs(count):
    return [pl.BlockSpec(memory_space=VMEM) for _ in range(count)]


def near(array):
    return pltpu.with_memory_space_constraint(array, VMEM)


def far(array):
    return pltpu.with_memory_space_constraint(array, pltpu.HBM)


def pack_kernel(k_ref, v_ref, dk_ref, dv_ref, *outs):
    for i, out in enumerate(outs):
        cols = slice(i * HEAD_DIM, (i + 1) * HEAD_DIM)
        for j, ref in enumerate((k_ref, v_ref, dk_ref, dv_ref)):
            out[j] = ref[:, cols]


def pick_kernel(own_ref, back_ref, out_ref):
    x = lax.axis_index("seq") % INNER

    @pl.when(x == 0)
    def _():
        out_ref[...] = own_ref[...]

    @pl.when(x != 0)
    def _():
        out_ref[...] = back_ref[...]


def attend_kernel(order, groups, lengths_ref, q_ref, dq_ref, *refs):
    owns, backs, near_ref, out_ref = refs[:groups], refs[groups:2 * groups], refs[-2], refs[-1]
    tok, width = out_ref.shape
    scale = HEAD_DIM ** (-0.5)
    shard = lax.axis_index("seq")
    group = (shard % INNER + 1 + order) % groups
    qpos = shard * tok + lax.broadcasted_iota(jnp.int32, (tok, tok), 0)
    lane = lax.broadcasted_iota(jnp.int32, (tok, tok), 1)
    begin = jnp.zeros((tok, tok), jnp.int32)
    end = jnp.int32(0)
    for i in range(lengths_ref.shape[1]):
        end = end + lengths_ref[0, i]
        begin = jnp.where(qpos >= end, jnp.maximum(begin, end), begin)
    biases = []
    for hop in range(DOC_SHARDS + 1):
        kpos = (shard - hop) * tok + lane
        allowed = (kpos >= begin) & (kpos <= qpos)
        biases.append(jnp.where(allowed, 0.0, -1e30).astype(F32))
    bias = jnp.concatenate(biases, axis=1)
    own = jnp.where(group == 0, owns[0][...], owns[1][...])
    back = jnp.where(group == 0, backs[0][...], backs[1][...])
    blocks = (own, near_ref, back)
    keys = jnp.concatenate([b[0] for b in blocks], axis=0)
    values = jnp.concatenate([b[1] for b in blocks], axis=0)
    dkeys = jnp.concatenate([b[2] for b in blocks], axis=0)
    dvalues = jnp.concatenate([b[3] for b in blocks], axis=0)
    both_keys = jnp.concatenate([keys, dkeys], axis=1)
    both_values = jnp.concatenate([values, dvalues], axis=0)
    for r in range(width // HEAD_DIM):
        cols = pl.ds(pl.multiple_of(group * width + r * HEAD_DIM, HEAD_DIM), HEAD_DIM)
        q, dq = q_ref[:, cols], dq_ref[:, cols]
        scores = nt_dot(q, keys) * scale + bias
        tangent = nt_dot(jnp.concatenate([dq, q], axis=1), both_keys) * scale
        weight = jnp.exp(scores - jnp.max(scores, axis=1, keepdims=True))
        weighted = weight * tangent
        total = jnp.sum(weight, axis=1, keepdims=True)
        cross = jnp.sum(weighted, axis=1, keepdims=True)
        low = weight.astype(BF16)
        accum = nn_dot(low, values)
        accum_tangent = nn_dot(jnp.concatenate([weighted.astype(BF16), low], axis=1), both_values)
        out = accum_tangent / total - (cross / total) * (accum / total)
        out_ref[:, r * HEAD_DIM:(r + 1) * HEAD_DIM] = out.astype(BF16)


def turn_kernel(cot_ref, q_ref, dq_ref, *outs):
    outs, (near_q, near_dq, sems) = outs[:-3], outs[-3:]
    fetches = [pltpu.make_async_copy(q_ref, near_q, sems.at[0]), pltpu.make_async_copy(dq_ref, near_dq, sems.at[1])]
    for fetch in fetches:
        fetch.start()
    outer = len(outs)
    share = outs[0].shape[0]
    parts = lax.axis_size("head")
    z, part = lax.axis_index("seq") // INNER, lax.axis_index("head")
    for k in range(outer):
        first = ((z ^ k) * parts + part) * share
        outs[k][...] = cot_ref[:, pl.ds(pl.multiple_of(first, 128), share)].T
    for fetch in fetches:
        fetch.wait()


def join_kernel(*refs):
    out_ref = refs[-1]
    for i, piece in enumerate(refs[:-1]):
        tok = piece.shape[1]
        out_ref[:, i * tok:(i + 1) * tok] = piece[...]


def merge_kernel(own_ref, got_ref, *outs):
    tok = own_ref.shape[0]
    for j, out in enumerate(outs):
        width = out.shape[1]
        out[:tok] = own_ref[:, j * width:(j + 1) * width]
        out[tok:] = got_ref[:, j * width:(j + 1) * width]


def project_kernel(shift, step, first_ref, last_ref, weight_ref, *refs):
    others, (out_ref, near_ref, sems) = refs[:-3], refs[-3:]
    rows, cols = near_ref.shape
    width = first_ref.shape[1]
    groups = rows // width
    x = lax.axis_index("seq") % INNER
    part = (lax.axis_index("head") + shift) % lax.axis_size("head")
    fetches = []
    for i in range(cols // step):
        at = pl.multiple_of(part * cols + i * step, 128)
        fetches.append(
            pltpu.make_async_copy(weight_ref.at[:, pl.ds(at, step)], near_ref.at[:, i * step:(i + 1) * step], sems.at[i])
        )
        fetches[-1].start()
    for i, fetch in enumerate(fetches):
        fetch.wait()
        here = slice(i * step, (i + 1) * step)
        out = None
        for j, dout in enumerate((first_ref, last_ref)):
            at = pl.multiple_of(((x + 1 + j) % groups) * width, width)
            term = nn_dot(dout[...], near_ref[pl.ds(at, width), here])
            out = term if out is None else out + term
        for other in others:
            out = out + other[:, here].astype(F32)
        out_ref[:, here] = out.astype(out_ref.dtype)


def product_kernel(shifts, folded, *refs):
    cots = refs[:4 * INNER]
    all_ref = refs[-1]
    pieces, outs = refs[4 * INNER:-len(shifts) - 1], refs[-len(shifts) - 1:-1]
    count = lax.axis_size("dp")
    x, own, part = lax.axis_index("seq") % INNER, lax.axis_index("dp"), lax.axis_index("head")
    z = lax.axis_index("seq") // INNER
    blocks = [p[...] for p in pieces]
    if folded:
        edge = (z == 0) | (z == 3)
        blocks = blocks[:3] + [jnp.where(edge, blocks[4], blocks[3])]
    tok = pieces[0].shape[0] // INNER
    half_count = len(blocks) // 2
    douts = []
    for e in range(INNER):
        for i in range(2):
            own_blocks = blocks[i * half_count:(i + 1) * half_count]
            douts.append(jnp.concatenate([b[e * tok:(e + 1) * tok] for b in own_blocks], axis=0))
    dout = jnp.concatenate(douts, axis=0)
    rows = outs[0].shape[0]
    half = cots[0].shape[0]
    for i in range(2):
        cot = jnp.concatenate([c[...] for c in cots[i * 2 * INNER:(i + 1) * 2 * INNER]], axis=1)
        at = pl.multiple_of(((part + i) % 2) * half, 128)
        all_ref[pl.ds(at, half), :] = nn_dot(cot, dout)
    for (dx, dy), out in zip(shifts, outs):
        at = pl.multiple_of((((x + dx) % INNER) * count + (own + dy) % count) * rows, 16)
        out[...] = all_ref[pl.ds(at, rows), :].astype(out.dtype)


def finish_kernel(*refs):
    out_ref = refs[-1]
    each = (len(refs) - 1) // CHUNKS
    x = lax.axis_index("seq") % INNER
    span = out_ref.shape[1] // INNER
    for j in range(CHUNKS):
        mine = refs[j * each:(j + 1) * each]
        side = each // INNER
        for dx in range(INNER):
            out = mine[dx * side][...].astype(F32)
            for other in mine[dx * side + 1:(dx + 1) * side]:
                out = out + other[...].astype(F32)
            width = out.shape[1]
            group = (x - dx) % INNER
            at = pl.multiple_of(group * span + j * width, 128)
            out_ref[:, pl.ds(at, width)] = out


def on_device(queries, keys, values, query_tangent, key_tangent, value_tangent, lengths, out_weight, cotangent):
    tok = queries.shape[1]
    seq_count, dp_count, head_count = (lax.axis_size(a) for a in ("seq", "dp", "head"))
    outer = seq_count // INNER
    groups = keys.shape[2] // HEAD_DIM
    width = queries.shape[2] // groups
    model = out_weight.shape[1]
    assert groups == INNER and head_count == INNER

    def call(kernel, shapes, *args, given=0, scratch=()):
        args = args[:given] + tuple(near(a) for a in args[given:])
        return pl.pallas_call(
            kernel,
            out_shape=[s if isinstance(s, jax.ShapeDtypeStruct) else VMEM(*s) for s in shapes],
            in_specs=specs(len(args)),
            out_specs=specs(len(shapes)),
            scratch_shapes=scratch,
            compiler_params=PARAMS,
        )(*args)

    def outward(block, k):
        return lax.ppermute(block, "seq", [(i, i ^ (k * INNER)) for i in range(seq_count)])

    def across(block):
        return lax.ppermute(block, "seq", [(i, i // INNER * INNER + (i + 1) % INNER) for i in range(seq_count)])

    def aside(block, s):
        return lax.ppermute(block, "head", [(i, (i + s) % head_count) for i in range(head_count)])

    def to_owner(block, dx, dy):
        perm = []
        for i in range(seq_count):
            for d in range(dp_count):
                to = i // INNER * INNER + (i + dx) % INNER
                perm.append((i * dp_count + d, to * dp_count + (d + dy) % dp_count))
        return lax.ppermute(block, ("seq", "dp"), perm)

    packed = call(pack_kernel, [((4, tok, HEAD_DIM), BF16)] * groups, *(far(a[0]) for a in (keys, values, key_tangent, value_tangent)), given=4)
    hop = [(i, i + INNER) for i in range(seq_count - INNER)]
    backs = {g: lax.ppermute(packed[g], "seq", hop) for g in reversed(range(groups))}
    nears = []
    for i in range(groups):
        (picked,) = call(pick_kernel, [((4, tok, HEAD_DIM), BF16)], packed[i], backs[1 - i])
        nears.append(across(picked))

    share = model // (outer * head_count)
    *turned, near_q, near_dq = pl.pallas_call(
        turn_kernel,
        out_shape=[VMEM((share, tok), BF16)] * outer + [VMEM((tok, width * groups), BF16)] * 2,
        in_specs=specs(1) + [pl.BlockSpec(memory_space=pltpu.HBM)] * 2,
        out_specs=specs(outer + 2),
        scratch_shapes=[pltpu.SemaphoreType.DMA((2,))],
        compiler_params=PARAMS,
        name="turn",
    )(far(cotangent[0]), far(queries[0]), far(query_tangent[0]))
    arrived = [turned[0]] + [outward(turned[k], k) for k in range(1, outer)]
    owns, nexts = [], []
    for i in range(2):
        segment = arrived[i * outer // 2:(i + 1) * outer // 2]
        owns += call(join_kernel, [((share, tok * len(segment)), BF16)], *segment)
        nexts.append(across(owns[i]))
    cots = [*owns, *nexts]
    cots += [aside(c, 1) for c in cots]

    douts = []
    for i in range(groups):
        douts.append(
            pl.pallas_call(
                functools.partial(attend_kernel, i, groups),
                out_shape=VMEM((tok, width), BF16),
                in_specs=[pl.BlockSpec(memory_space=pltpu.SMEM)] + specs(3 + 2 * groups),
                out_specs=specs(1)[0],
                compiler_params=PARAMS,
            )(far(lengths), near(near_q), near(near_dq), *(near(b) for b in (*packed, backs[0], backs[1], nears[i])))
        )
    got = across(douts[0])
    merged = call(merge_kernel, [((INNER * tok, width // CHUNKS), BF16)] * CHUNKS, douts[1], got)
    folded = outer == 4
    pieces = []
    for j in range(CHUNKS):
        came = [outward(merged[j], k) for k in range(1, outer - folded)]
        if folded:
            middle = [(z * INNER + x, (z ^ 3) * INNER + x) for z in (1, 2) for x in range(INNER)]
            ends = [(z * INNER + x, (z ^ 1) * INNER + x) for z in (1, 2) for x in range(INNER)]
            came.append(lax.ppermute(merged[j], "seq", middle))
            came.append(lax.ppermute(came[1], "seq", ends))
        pieces.append([merged[j]] + came)

    out_cols = model // head_count
    step = 512 if out_cols % 512 == 0 else out_cols
    blocks = out_cols // step

    def project(shift, space, others):
        return pl.pallas_call(
            functools.partial(project_kernel, shift, step),
            out_shape=space((tok, out_cols), BF16),
            in_specs=specs(groups) + [pl.BlockSpec(memory_space=pltpu.HBM)] + specs(len(others)),
            out_specs=specs(1)[0],
            scratch_shapes=[VMEM((width * groups, out_cols), BF16), pltpu.SemaphoreType.DMA((blocks,))],
            compiler_params=PARAMS,
        )(*(near(d) for d in douts), far(out_weight), *(near(o) for o in others))

    others = [aside(project(1, VMEM, []), 1)]
    layer_tangent = project(0, jax.ShapeDtypeStruct, others)

    rows = model // (seq_count * dp_count)
    order = [(dx, dy) for dx in reversed(range(INNER)) for dy in reversed(range(dp_count)) if dx or dy]
    parts = []
    for j in range(CHUNKS):
        shape = (rows, width // CHUNKS)
        *sent, mine = call(
            functools.partial(product_kernel, order + [(0, 0)], folded),
            [(shape, BF16)] * len(order) + [(shape, F32)],
            *cots,
            *pieces[j],
            scratch=[VMEM((share * head_count, width // CHUNKS), F32)],
        )
        came = {at: to_owner(block, *at) for at, block in zip(order, sent)}
        came[(0, 0)] = mine
        parts += [came[(dx, dy)] for dx in range(INNER) for dy in range(dp_count)]
    (weight_hvp,) = call(finish_kernel, [jax.ShapeDtypeStruct((rows, width * groups), F32)], *parts)
    return (layer_tangent[None], weight_hvp)


def solution(mesh):
    placed = (
        P("dp", "seq", "head"),
        P("dp", "seq", "head"),
        P("dp", "seq", "head"),
        P("dp", "seq", "head"),
        P("dp", "seq", "head"),
        P("dp", "seq", "head"),
        P("dp", None),
        P("head", None),
        P("dp", "seq", None),
    )

    return jax.shard_map(
        on_device,
        mesh=mesh,
        in_specs=placed,
        out_specs=(P("dp", "seq", "head"), P(("seq", "dp"), "head")),
        check_vma=False,
    )
```

```python
import functools

import jax
import jax.numpy as jnp
from jax import lax
from jax.experimental import pallas as pl
from jax.experimental.pallas import tpu as pltpu
from jax.sharding import PartitionSpec as P

HEAD_DIM = 128
DOC_SHARDS = 2
INNER = 2
CHUNKS = 2


BF16 = jnp.bfloat16
F32 = jnp.float32
VMEM = pltpu.VMEM
PARAMS = pltpu.CompilerParams(vmem_limit_bytes=12 * 1024 * 1024)


def nt_dot(a, b):
    return lax.dot_general(a, b, (((1,), (1,)), ((), ())), preferred_element_type=F32)


def nn_dot(a, b):
    return lax.dot_general(a, b, (((1,), (0,)), ((), ())), preferred_element_type=F32)


def specs(count):
    return [pl.BlockSpec(memory_space=VMEM) for _ in range(count)]


def near(array):
    return pltpu.with_memory_space_constraint(array, VMEM)


def far(array):
    return pltpu.with_memory_space_constraint(array, pltpu.HBM)


def pack_kernel(k_ref, v_ref, dk_ref, dv_ref, *outs):
    for i, out in enumerate(outs):
        cols = slice(i * HEAD_DIM, (i + 1) * HEAD_DIM)
        for j, ref in enumerate((k_ref, v_ref, dk_ref, dv_ref)):
            out[j] = ref[:, cols]


def pick_kernel(own_ref, back_ref, out_ref):
    x = lax.axis_index("seq") % INNER

    @pl.when(x == 0)
    def _():
        out_ref[...] = own_ref[...]

    @pl.when(x != 0)
    def _():
        out_ref[...] = back_ref[...]


def start_rows(source, first, span, target, sems):
    deep = target.shape[0] // sems.shape[0]
    fetches = []
    for i in range(sems.shape[0]):
        rows = source.at[first + i * deep:first + (i + 1) * deep, span]
        fetches.append(pltpu.make_async_copy(rows, target.at[i * deep:(i + 1) * deep], sems.at[i]))
        fetches[-1].start()
    return fetches


def attend_kernel(chunk, groups, bias_ref, q_ref, dq_ref, weight_ref, *refs):
    owns, backs, nears = (refs[i * groups:(i + 1) * groups] for i in range(3))
    outs, near_weight, sems = refs[3 * groups:4 * groups], refs[-2], refs[-1]
    cols = near_weight.shape[1]
    other = (lax.axis_index("head") + 1) % lax.axis_size("head")
    span = pl.ds(pl.multiple_of(other * cols, 128), cols)
    fetches = start_rows(weight_ref, chunk * near_weight.shape[0], span, near_weight, sems)
    tok, width = outs[0].shape
    scale = HEAD_DIM ** (-0.5)
    shard = lax.axis_index("seq")
    bias = bias_ref[...]
    for i in range(groups):
        group = (shard % INNER + i) % groups
        own = jnp.where(group == 0, owns[0][...], owns[1][...])
        back = jnp.where(group == 0, backs[0][...], backs[1][...])
        blocks = (own, nears[i], back)
        keys = jnp.concatenate([b[0] for b in blocks], axis=0)
        values = jnp.concatenate([b[1] for b in blocks], axis=0)
        dkeys = jnp.concatenate([b[2] for b in blocks], axis=0)
        dvalues = jnp.concatenate([b[3] for b in blocks], axis=0)
        both_keys = jnp.concatenate([keys, dkeys], axis=1)
        both_values = jnp.concatenate([values, dvalues], axis=0)
        at = pl.multiple_of((group * CHUNKS + chunk) * width, HEAD_DIM)
        q_all, dq_all = q_ref[:, pl.ds(at, width)], dq_ref[:, pl.ds(at, width)]
        heads = [slice(r * HEAD_DIM, (r + 1) * HEAD_DIM) for r in range(width // HEAD_DIM)]
        q = jnp.concatenate([q_all[:, h] for h in heads], axis=0)
        dq = jnp.concatenate([dq_all[:, h] for h in heads], axis=0)
        scores = nt_dot(q, keys) * scale + jnp.concatenate([bias] * len(heads), axis=0)
        tangent = nt_dot(jnp.concatenate([dq, q], axis=1), both_keys) * scale
        weight = jnp.exp(scores - jnp.max(scores, axis=1, keepdims=True))
        weighted = weight * tangent
        total = jnp.sum(weight, axis=1, keepdims=True)
        cross = jnp.sum(weighted, axis=1, keepdims=True)
        low = weight.astype(BF16)
        accum = nn_dot(low, values)
        accum_tangent = nn_dot(jnp.concatenate([weighted.astype(BF16), low], axis=1), both_values)
        out = (accum_tangent / total - (cross / total) * (accum / total)).astype(BF16)
        for r, h in enumerate(heads):
            outs[i][:, h] = out[r * tok:(r + 1) * tok]
    for fetch in fetches:
        fetch.wait()


def turn_kernel(lengths_ref, cot_ref, q_ref, dq_ref, *outs):
    outs, (near_q, near_dq, bias_ref, sems) = outs[:-4], outs[-4:]
    fetches = [pltpu.make_async_copy(q_ref, near_q, sems.at[0]), pltpu.make_async_copy(dq_ref, near_dq, sems.at[1])]
    for fetch in fetches:
        fetch.start()
    outer = len(outs)
    share = outs[0].shape[0]
    parts = lax.axis_size("head")
    z, part = lax.axis_index("seq") // INNER, lax.axis_index("head")
    for k in range(outer):
        first = ((z ^ k) * parts + part) * share
        outs[k][...] = cot_ref[:, pl.ds(pl.multiple_of(first, 128), share)].T
    tok = q_ref.shape[0]
    shard = lax.axis_index("seq")
    qpos = shard * tok + lax.broadcasted_iota(jnp.int32, (tok, tok), 0)
    lane = lax.broadcasted_iota(jnp.int32, (tok, tok), 1)
    begin = jnp.zeros((tok, tok), jnp.int32)
    end = jnp.int32(0)
    for i in range(lengths_ref.shape[1]):
        end = end + lengths_ref[0, i]
        begin = jnp.where(qpos >= end, jnp.maximum(begin, end), begin)
    biases = []
    for hop in range(DOC_SHARDS + 1):
        kpos = (shard - hop) * tok + lane
        allowed = (kpos >= begin) & (kpos <= qpos)
        biases.append(jnp.where(allowed, 0.0, -1e30).astype(F32))
    bias_ref[...] = jnp.concatenate(biases, axis=1)
    for fetch in fetches:
        fetch.wait()


def join_kernel(*refs):
    out_ref = refs[-1]
    for i, piece in enumerate(refs[:-1]):
        tok = piece.shape[1]
        out_ref[:, i * tok:(i + 1) * tok] = piece[...]


def merge_kernel(own_ref, got_ref, out_ref):
    tok = own_ref.shape[0]
    out_ref[:tok] = own_ref[...]
    out_ref[tok:] = got_ref[...]


def in_order(douts, x):
    out = []
    for i in range(len(douts)):
        group, chunk = i // CHUNKS, i % CHUNKS
        out.append(jnp.where(x == group, douts[chunk * INNER][...], douts[chunk * INNER + 1][...]))
    return out


def given_kernel(count, *refs):
    weights, out_ref = refs[count:-1], refs[-1]
    douts = in_order(refs[:count], lax.axis_index("seq") % INNER)
    each = count // len(weights)
    out = None
    for i, weight in enumerate(weights):
        term = nn_dot(jnp.concatenate(douts[i * each:(i + 1) * each], axis=1), weight[...])
        out = term if out is None else out + term
    out_ref[...] = out.astype(out_ref.dtype)


def kept_kernel(count, *refs):
    weight_ref, other_ref, out_ref, near_weight, sems = refs[count:]
    cols = near_weight.shape[1]
    span = pl.ds(pl.multiple_of(lax.axis_index("head") * cols, 128), cols)
    fetches = start_rows(weight_ref, 0, span, near_weight, sems)
    douts = in_order(refs[:count], lax.axis_index("seq") % INNER)
    width = douts[0].shape[1]
    out = other_ref[...].astype(F32)
    for i, dout in enumerate(douts):
        for fetch in fetches[i * len(fetches) // count:(i + 1) * len(fetches) // count]:
            fetch.wait()
        out = out + nn_dot(dout, near_weight[i * width:(i + 1) * width, :])
    out_ref[...] = out.astype(out_ref.dtype)


def product_kernel(shifts, *refs):
    cots = refs[:4 * INNER]
    all_ref = refs[-1]
    pieces, outs = refs[4 * INNER:-len(shifts) - 1], refs[-len(shifts) - 1:-1]
    count = lax.axis_size("dp")
    x, own, part = lax.axis_index("seq") % INNER, lax.axis_index("dp"), lax.axis_index("head")
    tok = pieces[0].shape[0] // INNER
    douts = [p[e * tok:(e + 1) * tok] for e in range(INNER) for p in pieces]
    dout = jnp.concatenate(douts, axis=0)
    rows = outs[0].shape[0]
    half = cots[0].shape[0]
    for i in range(2):
        cot = jnp.concatenate([c[...] for c in cots[i * 2 * INNER:(i + 1) * 2 * INNER]], axis=1)
        at = pl.multiple_of(((part + i) % 2) * half, 128)
        all_ref[pl.ds(at, half), :] = nn_dot(cot, dout)
    for (dx, dy), out in zip(shifts, outs):
        at = pl.multiple_of((((x + dx) % INNER) * count + (own + dy) % count) * rows, 16)
        out[...] = all_ref[pl.ds(at, rows), :].astype(out.dtype)


def finish_kernel(*refs):
    out_ref = refs[-1]
    each = (len(refs) - 1) // CHUNKS
    x = lax.axis_index("seq") % INNER
    span = out_ref.shape[1] // INNER
    for j in range(CHUNKS):
        mine = refs[j * each:(j + 1) * each]
        side = each // INNER
        for dx in range(INNER):
            out = mine[dx * side][...].astype(F32)
            for other in mine[dx * side + 1:(dx + 1) * side]:
                out = out + other[...].astype(F32)
            width = out.shape[1]
            group = (x - dx) % INNER
            at = pl.multiple_of(group * span + j * width, 128)
            out_ref[:, pl.ds(at, width)] = out


def on_device(queries, keys, values, query_tangent, key_tangent, value_tangent, lengths, out_weight, cotangent):
    tok = queries.shape[1]
    seq_count, dp_count, head_count = (lax.axis_size(a) for a in ("seq", "dp", "head"))
    outer = seq_count // INNER
    groups = keys.shape[2] // HEAD_DIM
    width = queries.shape[2] // groups
    model = out_weight.shape[1]
    assert groups == INNER and head_count == INNER

    def call(kernel, shapes, *args, given=0, scratch=()):
        args = args[:given] + tuple(near(a) for a in args[given:])
        return pl.pallas_call(
            kernel,
            out_shape=[VMEM(*s) if isinstance(s, tuple) else s for s in shapes],
            in_specs=specs(len(args)),
            out_specs=specs(len(shapes)),
            scratch_shapes=scratch,
            compiler_params=PARAMS,
        )(*args)

    def outward(block, k):
        return lax.ppermute(block, "seq", [(i, i ^ (k * INNER)) for i in range(seq_count)])

    def across(block):
        return lax.ppermute(block, "seq", [(i, i // INNER * INNER + (i + 1) % INNER) for i in range(seq_count)])

    def aside(block, s):
        return lax.ppermute(block, "head", [(i, (i + s) % head_count) for i in range(head_count)])

    def to_owner(block, dx, dy):
        perm = []
        for i in range(seq_count):
            for d in range(dp_count):
                to = i // INNER * INNER + (i + dx) % INNER
                perm.append((i * dp_count + d, to * dp_count + (d + dy) % dp_count))
        return lax.ppermute(block, ("seq", "dp"), perm)

    packed = call(pack_kernel, [((4, tok, HEAD_DIM), BF16)] * groups, *(far(a[0]) for a in (keys, values, key_tangent, value_tangent)), given=4)
    hop = [(i, (i + INNER) % seq_count) for i in range(seq_count)]
    backs = {g: lax.ppermute(packed[g], "seq", hop) for g in range(groups)}
    nears = []
    for i in range(groups):
        (picked,) = call(pick_kernel, [((4, tok, HEAD_DIM), BF16)], packed[1 - i], backs[i])
        nears.append(across(picked))

    share = model // (outer * head_count)
    *turned, near_q, near_dq, bias = pl.pallas_call(
        turn_kernel,
        out_shape=[VMEM((share, tok), BF16)] * outer + [VMEM((tok, width * groups), BF16)] * 2
        + [VMEM((tok, tok * (DOC_SHARDS + 1)), F32)],
        in_specs=[pl.BlockSpec(memory_space=pltpu.SMEM)] + specs(1) + [pl.BlockSpec(memory_space=pltpu.HBM)] * 2,
        out_specs=specs(outer + 3),
        scratch_shapes=[pltpu.SemaphoreType.DMA((2,))],
        compiler_params=PARAMS,
        name="turn",
    )(far(lengths), far(cotangent[0]), far(queries[0]), far(query_tangent[0]))
    arrived = [turned[0]] + [outward(turned[k], k) for k in range(1, outer)]
    owns, nexts = [], []
    for i in range(2):
        segment = arrived[i * outer // 2:(i + 1) * outer // 2]
        owns += call(join_kernel, [((share, tok * len(segment)), BF16)], *segment)
        nexts.append(across(owns[i]))
    cots = [*owns, *nexts]
    cots += [aside(c, 1) for c in cots]

    out_cols = model // head_count
    douts, weights = [], []
    for j in range(CHUNKS):
        *two, near_weight = pl.pallas_call(
            functools.partial(attend_kernel, j, groups),
            out_shape=[VMEM((tok, width // CHUNKS), BF16)] * groups + [VMEM((width * groups // CHUNKS, out_cols), BF16)],
            in_specs=[*specs(3), pl.BlockSpec(memory_space=pltpu.HBM)]
            + specs(3 * groups),
            out_specs=specs(groups + 1),
            scratch_shapes=[pltpu.SemaphoreType.DMA((4,))],
            compiler_params=PARAMS,
        )(
            near(bias),
            near(near_q),
            near(near_dq),
            far(out_weight),
            *(near(b) for b in (*packed, backs[0], backs[1], *nears)),
        )
        douts += two
        weights.append(near_weight)

    def gather(block):
        held = {0: block}
        step = outer // 2
        while step:
            held.update({k + step: outward(b, step) for k, b in held.items()})
            step //= 2
        return [held[k] for k in range(outer)]

    pieces = []
    for j in range(CHUNKS):
        mine, other = douts[j * groups:(j + 1) * groups]
        shape = ((INNER * tok, width // CHUNKS), BF16)
        (merged,) = call(merge_kernel, [shape], mine, across(other))
        pieces.append(gather(merged))

    (given,) = call(functools.partial(given_kernel, len(douts)), [((tok, out_cols), BF16)], *douts, *weights)
    got = aside(given, 1)
    layer_tangent = pl.pallas_call(
        functools.partial(kept_kernel, len(douts)),
        out_shape=jax.ShapeDtypeStruct((tok, out_cols), BF16),
        in_specs=specs(len(douts)) + [pl.BlockSpec(memory_space=pltpu.HBM)] + specs(1),
        out_specs=specs(1)[0],
        scratch_shapes=[VMEM((width * groups, out_cols), BF16), pltpu.SemaphoreType.DMA((8,))],
        compiler_params=PARAMS,
        name="kept",
    )(*(near(d) for d in douts), far(out_weight), near(got))

    rows = model // (seq_count * dp_count)
    order = [(dx, dy) for dx in reversed(range(INNER)) for dy in reversed(range(dp_count)) if dx or dy]
    parts = []
    for j in range(CHUNKS):
        shape = (rows, width // CHUNKS)
        *sent, mine = call(
            functools.partial(product_kernel, order + [(0, 0)]),
            [(shape, BF16)] * len(order) + [(shape, F32)],
            *cots,
            *pieces[j],
            scratch=[VMEM((share * head_count, width // CHUNKS), F32)],
        )
        came = {at: to_owner(block, *at) for at, block in zip(order, sent)}
        came[(0, 0)] = mine
        parts += [came[(dx, dy)] for dx in range(INNER) for dy in range(dp_count)]
    (weight_hvp,) = call(finish_kernel, [jax.ShapeDtypeStruct((rows, width * groups), F32)], *parts)
    return (layer_tangent[None], weight_hvp)


def solution(mesh):
    placed = (
        P("dp", "seq", "head"),
        P("dp", "seq", "head"),
        P("dp", "seq", "head"),
        P("dp", "seq", "head"),
        P("dp", "seq", "head"),
        P("dp", "seq", "head"),
        P("dp", None),
        P("head", None),
        P("dp", "seq", None),
    )

    return jax.shard_map(
        on_device,
        mesh=mesh,
        in_specs=placed,
        out_specs=(P("dp", "seq", "head"), P(("seq", "dp"), "head")),
        check_vma=False,
    )
```

```python
import functools

import jax
import jax.numpy as jnp
from jax import lax
from jax.experimental import pallas as pl
from jax.experimental.pallas import tpu as pltpu
from jax.sharding import PartitionSpec as P

HEAD_DIM = 128
DOC_SHARDS = 2
INNER = 2
CHUNKS = 2


BF16 = jnp.bfloat16
F32 = jnp.float32
VMEM = pltpu.VMEM
PARAMS = pltpu.CompilerParams(vmem_limit_bytes=12 * 1024 * 1024)


def nt_dot(a, b):
    return lax.dot_general(a, b, (((1,), (1,)), ((), ())), preferred_element_type=F32)


def nn_dot(a, b):
    return lax.dot_general(a, b, (((1,), (0,)), ((), ())), preferred_element_type=F32)


def specs(count):
    return [pl.BlockSpec(memory_space=VMEM) for _ in range(count)]


def near(array):
    return pltpu.with_memory_space_constraint(array, VMEM)


def far(array):
    return pltpu.with_memory_space_constraint(array, pltpu.HBM)


def pack_kernel(k_ref, v_ref, dk_ref, dv_ref, own_ref, give_ref):
    x = lax.axis_index("seq") % INNER
    for out, group in ((own_ref, x), (give_ref, 1 - x)):
        cols = pl.ds(pl.multiple_of(group * HEAD_DIM, HEAD_DIM), HEAD_DIM)
        for j, ref in enumerate((k_ref, v_ref, dk_ref, dv_ref)):
            out[j] = ref[:, cols]


def pack_queries_kernel(q_ref, dq_ref, own_ref, give_ref):
    x = lax.axis_index("seq") % INNER
    width = own_ref.shape[2]
    for out, group in ((own_ref, x), (give_ref, 1 - x)):
        cols = pl.ds(pl.multiple_of(group * width, HEAD_DIM), width)
        out[0] = q_ref[:, cols]
        out[1] = dq_ref[:, cols]


def start_rows(source, first, span, target, sems):
    deep = target.shape[0] // sems.shape[0]
    fetches = []
    for i in range(sems.shape[0]):
        rows = source.at[first + i * deep:first + (i + 1) * deep, span]
        fetches.append(pltpu.make_async_copy(rows, target.at[i * deep:(i + 1) * deep], sems.at[i]))
        fetches[-1].start()
    return fetches


def attend_kernel(chunk, bias_ref, own_q, other_q, weight_ref, own_kv, other_kv, own_back, other_back, *refs):
    out_ref, give_ref, near_weight, sems = refs[-4:]
    cols = near_weight.shape[1]
    other = (lax.axis_index("head") + 1) % lax.axis_size("head")
    span = pl.ds(pl.multiple_of(other * cols, 128), cols)
    fetches = start_rows(weight_ref, chunk * near_weight.shape[0], span, near_weight, sems)
    tok, width = out_ref.shape[0] // INNER, out_ref.shape[1]
    scale = HEAD_DIM ** (-0.5)
    x = lax.axis_index("seq") % INNER
    places = (
        (own_q, own_kv[...], own_back[...], jnp.where(x == 1, other_kv[...], other_back[...])),
        (other_q, other_kv[...], other_back[...], jnp.where(x == 0, own_kv[...], own_back[...])),
    )
    heads = [slice(r * HEAD_DIM, (r + 1) * HEAD_DIM) for r in range(width // HEAD_DIM)]
    for e, (q_ref, *blocks) in enumerate(places):
        bias = bias_ref[e]
        keys = jnp.concatenate([b[0] for b in blocks], axis=0)
        values = jnp.concatenate([b[1] for b in blocks], axis=0)
        dkeys = jnp.concatenate([b[2] for b in blocks], axis=0)
        dvalues = jnp.concatenate([b[3] for b in blocks], axis=0)
        both_keys = jnp.concatenate([keys, dkeys], axis=1)
        both_values = jnp.concatenate([values, dvalues], axis=0)
        here = slice(chunk * width, (chunk + 1) * width)
        q_all, dq_all = q_ref[0, :, here], q_ref[1, :, here]
        q = jnp.concatenate([q_all[:, h] for h in heads], axis=0)
        dq = jnp.concatenate([dq_all[:, h] for h in heads], axis=0)
        scores = nt_dot(q, keys) * scale + jnp.concatenate([bias] * len(heads), axis=0)
        tangent = nt_dot(jnp.concatenate([dq, q], axis=1), both_keys) * scale
        weight = jnp.exp(scores - jnp.max(scores, axis=1, keepdims=True))
        weighted = weight * tangent
        total = jnp.sum(weight, axis=1, keepdims=True)
        cross = jnp.sum(weighted, axis=1, keepdims=True)
        low = weight.astype(BF16)
        accum = nn_dot(low, values)
        accum_tangent = nn_dot(jnp.concatenate([weighted.astype(BF16), low], axis=1), both_values)
        out = (accum_tangent / total - (cross / total) * (accum / total)).astype(BF16)
        for r, h in enumerate(heads):
            out_ref[e * tok:(e + 1) * tok, h] = out[r * tok:(r + 1) * tok]
            if e:
                give_ref[:, chunk * width + h.start:chunk * width + h.stop] = out[r * tok:(r + 1) * tok]
    if chunk:
        give_ref[:, :chunk * width] = refs[0][:, :chunk * width]
    for fetch in fetches:
        fetch.wait()


def turn_kernel(lengths_ref, cot_ref, *outs):
    outs, bias_ref = outs[:-1], outs[-1]
    outer = len(outs)
    share = outs[0].shape[0]
    parts = lax.axis_size("head")
    shard, part = lax.axis_index("seq"), lax.axis_index("head")
    z, x = shard // INNER, shard % INNER
    for k in range(outer):
        first = ((z ^ k) * parts + part) * share
        outs[k][...] = cot_ref[:, pl.ds(pl.multiple_of(first, 128), share)].T
    tok = bias_ref.shape[1]
    row = lax.broadcasted_iota(jnp.int32, (tok, tok), 0)
    lane = lax.broadcasted_iota(jnp.int32, (tok, tok), 1)
    for e in range(INNER):
        place = z * INNER + (x + e) % INNER
        qpos = place * tok + row
        begin = jnp.zeros((tok, tok), jnp.int32)
        end = jnp.int32(0)
        for i in range(lengths_ref.shape[1]):
            end = end + lengths_ref[0, i]
            begin = jnp.where(qpos >= end, jnp.maximum(begin, end), begin)
        for i, hop in enumerate((0, 2, 1)):
            kpos = (place - hop) * tok + lane
            allowed = (kpos >= begin) & (kpos <= qpos)
            bias_ref[e, :, i * tok:(i + 1) * tok] = jnp.where(allowed, 0.0, -1e30).astype(F32)


def join_kernel(*refs):
    out_ref = refs[-1]
    for i, piece in enumerate(refs[:-1]):
        tok = piece.shape[1]
        out_ref[:, i * tok:(i + 1) * tok] = piece[...]


def in_order(blocks, got_ref, x):
    tok, width = got_ref.shape[0], blocks[0].shape[1]
    out = []
    for group in range(INNER):
        for chunk, block in enumerate(blocks):
            out.append(jnp.where(x == group, block[:tok], got_ref[:, chunk * width:(chunk + 1) * width]))
    return out


def given_kernel(*refs):
    weights, out_ref = refs[CHUNKS + 1:-1], refs[-1]
    douts = in_order(refs[:CHUNKS], refs[CHUNKS], lax.axis_index("seq") % INNER)
    each = len(douts) // len(weights)
    out = None
    for i, weight in enumerate(weights):
        term = nn_dot(jnp.concatenate(douts[i * each:(i + 1) * each], axis=1), weight[...])
        out = term if out is None else out + term
    out_ref[...] = out.astype(out_ref.dtype)


def kept_kernel(*refs):
    weight_ref, other_ref, out_ref, near_weight, sems = refs[CHUNKS + 1:]
    cols = near_weight.shape[1]
    span = pl.ds(pl.multiple_of(lax.axis_index("head") * cols, 128), cols)
    fetches = start_rows(weight_ref, 0, span, near_weight, sems)
    douts = in_order(refs[:CHUNKS], refs[CHUNKS], lax.axis_index("seq") % INNER)
    count, width = len(douts), douts[0].shape[1]
    out = other_ref[...].astype(F32)
    for i, dout in enumerate(douts):
        for fetch in fetches[i * len(fetches) // count:(i + 1) * len(fetches) // count]:
            fetch.wait()
        out = out + nn_dot(dout, near_weight[i * width:(i + 1) * width, :])
    out_ref[...] = out.astype(out_ref.dtype)


def product_kernel(shifts, *refs):
    cots = refs[:2 * INNER]
    all_ref = refs[-1]
    pieces, outs = refs[2 * INNER:-len(shifts) - 1], refs[-len(shifts) - 1:-1]
    count = lax.axis_size("dp")
    x, own, part = lax.axis_index("seq") % INNER, lax.axis_index("dp"), lax.axis_index("head")
    tok = pieces[0].shape[0] // INNER
    douts = [p[e * tok:(e + 1) * tok] for e in range(INNER) for p in pieces]
    dout = jnp.concatenate(douts, axis=0)
    rows = outs[0].shape[0]
    half = cots[0].shape[0]
    for i in range(2):
        cot = jnp.concatenate([c[...] for c in cots[i * INNER:(i + 1) * INNER]], axis=1)
        at = pl.multiple_of(((part + i) % 2) * half, 128)
        all_ref[pl.ds(at, half), :] = nn_dot(cot, dout)
    for (dx, dy), out in zip(shifts, outs):
        at = pl.multiple_of((((x + dx) % INNER) * count + (own + dy) % count) * rows, 16)
        out[...] = all_ref[pl.ds(at, rows), :].astype(out.dtype)


def finish_kernel(*refs):
    out_ref = refs[-1]
    each = (len(refs) - 1) // CHUNKS
    x = lax.axis_index("seq") % INNER
    span = out_ref.shape[1] // INNER
    for j in range(CHUNKS):
        mine = refs[j * each:(j + 1) * each]
        side = each // INNER
        for dx in range(INNER):
            out = mine[dx * side][...].astype(F32)
            for other in mine[dx * side + 1:(dx + 1) * side]:
                out = out + other[...].astype(F32)
            width = out.shape[1]
            group = (x - dx) % INNER
            at = pl.multiple_of(group * span + j * width, 128)
            out_ref[:, pl.ds(at, width)] = out


def on_device(queries, keys, values, query_tangent, key_tangent, value_tangent, lengths, out_weight, cotangent):
    tok = queries.shape[1]
    seq_count, dp_count, head_count = (lax.axis_size(a) for a in ("seq", "dp", "head"))
    outer = seq_count // INNER
    groups = keys.shape[2] // HEAD_DIM
    width = queries.shape[2] // groups
    model = out_weight.shape[1]
    assert groups == INNER and head_count == INNER

    def call(kernel, shapes, *args, given=0, scratch=()):
        args = args[:given] + tuple(near(a) for a in args[given:])
        return pl.pallas_call(
            kernel,
            out_shape=[VMEM(*s) if isinstance(s, tuple) else s for s in shapes],
            in_specs=specs(len(args)),
            out_specs=specs(len(shapes)),
            scratch_shapes=scratch,
            compiler_params=PARAMS,
        )(*args)

    def outward(block, k):
        return lax.ppermute(block, "seq", [(i, i ^ (k * INNER)) for i in range(seq_count)])

    def across(block):
        return lax.ppermute(block, "seq", [(i, i // INNER * INNER + (i + 1) % INNER) for i in range(seq_count)])

    def aside(block, s):
        return lax.ppermute(block, "head", [(i, (i + s) % head_count) for i in range(head_count)])

    def to_owner(block, dx, dy):
        perm = []
        for i in range(seq_count):
            for d in range(dp_count):
                to = i // INNER * INNER + (i + dx) % INNER
                perm.append((i * dp_count + d, to * dp_count + (d + dy) % dp_count))
        return lax.ppermute(block, ("seq", "dp"), perm)

    kv_shape = ((4, tok, HEAD_DIM), BF16)
    own_kv, give_kv = call(
        pack_kernel, [kv_shape] * 2, *(far(a[0]) for a in (keys, values, key_tangent, value_tangent)), given=4
    )
    other_kv = across(give_kv)
    hop = [(i, (i + INNER) % seq_count) for i in range(seq_count)]
    own_back = lax.ppermute(own_kv, "seq", hop)
    other_back = lax.ppermute(other_kv, "seq", hop)
    q_shape = ((2, tok, width), BF16)
    own_q, give_q = call(pack_queries_kernel, [q_shape] * 2, far(queries[0]), far(query_tangent[0]), given=2)
    other_q = across(give_q)

    share = model // (outer * head_count)
    *turned, bias = pl.pallas_call(
        turn_kernel,
        out_shape=[VMEM((share, tok), BF16)] * outer + [VMEM((INNER, tok, tok * (DOC_SHARDS + 1)), F32)],
        in_specs=[pl.BlockSpec(memory_space=pltpu.SMEM)] + specs(1),
        out_specs=specs(outer + 1),
        compiler_params=PARAMS,
        name="turn",
    )(far(lengths), far(cotangent[0]))
    arrived = [turned[0]] + [outward(turned[k], k) for k in range(1, outer)]
    beside = [across(block) for block in arrived]
    joined = ((share, tok * outer), BF16)
    cots = [call(join_kernel, [joined], *blocks)[0] for blocks in (arrived, beside)]
    cots += [aside(cot, 1) for cot in cots]

    out_cols = model // head_count
    blocks, weights, give = [], [], []
    for j in range(CHUNKS):
        inputs = [bias, own_q, other_q, out_weight, own_kv, other_kv, own_back, other_back, *give]
        block, given_dout, near_weight = pl.pallas_call(
            functools.partial(attend_kernel, j),
            out_shape=[
                VMEM((INNER * tok, width // CHUNKS), BF16),
                VMEM((tok, width), BF16),
                VMEM((width * groups // CHUNKS, out_cols), BF16),
            ],
            in_specs=specs(3) + [pl.BlockSpec(memory_space=pltpu.HBM)] + specs(len(inputs) - 4),
            out_specs=specs(3),
            scratch_shapes=[pltpu.SemaphoreType.DMA((4,))],
            compiler_params=PARAMS,
        )(*(far(a) if i == 3 else near(a) for i, a in enumerate(inputs)))
        blocks.append(block)
        weights.append(near_weight)
        give = [given_dout]
    got = across(give[0])

    def gather(block):
        held = {0: block}
        step = outer // 2
        while step:
            held.update({k + step: outward(b, step) for k, b in held.items()})
            step //= 2
        return [held[k] for k in range(outer)]

    pieces = [gather(block) for block in blocks]

    (given,) = call(given_kernel, [((tok, out_cols), BF16)], *blocks, got, *weights)
    added = aside(given, 1)
    layer_tangent = pl.pallas_call(
        kept_kernel,
        out_shape=jax.ShapeDtypeStruct((tok, out_cols), BF16),
        in_specs=specs(CHUNKS + 1) + [pl.BlockSpec(memory_space=pltpu.HBM)] + specs(1),
        out_specs=specs(1)[0],
        scratch_shapes=[VMEM((width * groups, out_cols), BF16), pltpu.SemaphoreType.DMA((8,))],
        compiler_params=PARAMS,
        name="kept",
    )(*(near(b) for b in (*blocks, got)), far(out_weight), near(added))

    rows = model // (seq_count * dp_count)
    order = [(dx, dy) for dx in reversed(range(INNER)) for dy in reversed(range(dp_count)) if dx or dy]
    parts = []
    for j in range(CHUNKS):
        shape = (rows, width // CHUNKS)
        *sent, mine = call(
            functools.partial(product_kernel, order + [(0, 0)]),
            [(shape, BF16)] * len(order) + [(shape, F32)],
            *cots,
            *pieces[j],
            scratch=[VMEM((share * head_count, width // CHUNKS), F32)],
        )
        came = {at: to_owner(block, *at) for at, block in zip(order, sent)}
        came[(0, 0)] = mine
        parts += [came[(dx, dy)] for dx in range(INNER) for dy in range(dp_count)]
    (weight_hvp,) = call(finish_kernel, [jax.ShapeDtypeStruct((rows, width * groups), F32)], *parts)
    return (layer_tangent[None], weight_hvp)


def solution(mesh):
    placed = (
        P("dp", "seq", "head"),
        P("dp", "seq", "head"),
        P("dp", "seq", "head"),
        P("dp", "seq", "head"),
        P("dp", "seq", "head"),
        P("dp", "seq", "head"),
        P("dp", None),
        P("head", None),
        P("dp", "seq", None),
    )

    return jax.shard_map(
        on_device,
        mesh=mesh,
        in_specs=placed,
        out_specs=(P("dp", "seq", "head"), P(("seq", "dp"), "head")),
        check_vma=False,
    )
```

```python
import functools

import jax
import jax.numpy as jnp
from jax import lax
from jax.experimental import pallas as pl
from jax.experimental.pallas import tpu as pltpu
from jax.sharding import PartitionSpec as P

HEAD_DIM = 128
DOC_SHARDS = 2
INNER = 2
CHUNKS = 2


BF16 = jnp.bfloat16
F32 = jnp.float32
VMEM = pltpu.VMEM
PARAMS = pltpu.CompilerParams(vmem_limit_bytes=12 * 1024 * 1024)


def nt_dot(a, b):
    return lax.dot_general(a, b, (((1,), (1,)), ((), ())), preferred_element_type=F32)


def nn_dot(a, b):
    return lax.dot_general(a, b, (((1,), (0,)), ((), ())), preferred_element_type=F32)


def specs(count):
    return [pl.BlockSpec(memory_space=VMEM) for _ in range(count)]


def near(array):
    return pltpu.with_memory_space_constraint(array, VMEM)


def far(array):
    return pltpu.with_memory_space_constraint(array, pltpu.HBM)


def pack_kernel(k_ref, v_ref, dk_ref, dv_ref, own_ref, give_ref):
    x = lax.axis_index("seq") % INNER
    for out, group in ((own_ref, x), (give_ref, 1 - x)):
        cols = pl.ds(pl.multiple_of(group * HEAD_DIM, HEAD_DIM), HEAD_DIM)
        for j, ref in enumerate((k_ref, v_ref, dk_ref, dv_ref)):
            out[j] = ref[:, cols]


def pack_queries_kernel(q_ref, dq_ref, own_ref, give_ref):
    x = lax.axis_index("seq") % INNER
    width = own_ref.shape[2]
    for out, group in ((own_ref, x), (give_ref, 1 - x)):
        cols = pl.ds(pl.multiple_of(group * width, HEAD_DIM), width)
        out[0] = q_ref[:, cols]
        out[1] = dq_ref[:, cols]


def start_rows(source, first, span, target, sems):
    deep = target.shape[0] // sems.shape[0]
    fetches = []
    for i in range(sems.shape[0]):
        rows = source.at[first + i * deep:first + (i + 1) * deep, span]
        fetches.append(pltpu.make_async_copy(rows, target.at[i * deep:(i + 1) * deep], sems.at[i]))
        fetches[-1].start()
    return fetches


def attend_kernel(chunk, bias_ref, own_q, other_q, weight_ref, own_kv, other_kv, own_back, other_back, *refs):
    out_ref, give_ref, near_weight, sems = refs[-4:]
    cols = near_weight.shape[1]
    other = (lax.axis_index("head") + 1) % lax.axis_size("head")
    span = pl.ds(pl.multiple_of(other * cols, 128), cols)
    fetches = start_rows(weight_ref, chunk * near_weight.shape[0], span, near_weight, sems)
    tok, width = out_ref.shape[0] // INNER, out_ref.shape[1]
    scale = HEAD_DIM ** (-0.5)
    x = lax.axis_index("seq") % INNER
    places = (
        (own_q, own_kv[...], own_back[...], jnp.where(x == 1, other_kv[...], other_back[...])),
        (other_q, other_kv[...], other_back[...], jnp.where(x == 0, own_kv[...], own_back[...])),
    )
    heads = [slice(r * HEAD_DIM, (r + 1) * HEAD_DIM) for r in range(width // HEAD_DIM)]
    for e, (q_ref, *blocks) in enumerate(places):
        bias = bias_ref[e]
        keys = jnp.concatenate([b[0] for b in blocks], axis=0)
        values = jnp.concatenate([b[1] for b in blocks], axis=0)
        dkeys = jnp.concatenate([b[2] for b in blocks], axis=0)
        dvalues = jnp.concatenate([b[3] for b in blocks], axis=0)
        both_keys = jnp.concatenate([keys, dkeys], axis=1)
        both_values = jnp.concatenate([values, dvalues], axis=0)
        here = slice(chunk * width, (chunk + 1) * width)
        q_all, dq_all = q_ref[0, :, here], q_ref[1, :, here]
        q = jnp.concatenate([q_all[:, h] for h in heads], axis=0)
        dq = jnp.concatenate([dq_all[:, h] for h in heads], axis=0)
        scores = nt_dot(q, keys) * scale + jnp.concatenate([bias] * len(heads), axis=0)
        tangent = nt_dot(jnp.concatenate([dq, q], axis=1), both_keys) * scale
        weight = jnp.exp(scores - jnp.max(scores, axis=1, keepdims=True))
        weighted = weight * tangent
        total = jnp.sum(weight, axis=1, keepdims=True)
        cross = jnp.sum(weighted, axis=1, keepdims=True)
        low = weight.astype(BF16)
        accum = nn_dot(low, values)
        accum_tangent = nn_dot(jnp.concatenate([weighted.astype(BF16), low], axis=1), both_values)
        out = (accum_tangent / total - (cross / total) * (accum / total)).astype(BF16)
        for r, h in enumerate(heads):
            out_ref[e * tok:(e + 1) * tok, h] = out[r * tok:(r + 1) * tok]
            if e:
                give_ref[:, chunk * width + h.start:chunk * width + h.stop] = out[r * tok:(r + 1) * tok]
    if chunk:
        give_ref[:, :chunk * width] = refs[0][:, :chunk * width]
    for fetch in fetches:
        fetch.wait()


def turn_kernel(lengths_ref, cot_ref, *outs):
    outs, bias_ref = outs[:-1], outs[-1]
    outer = len(outs)
    share = outs[0].shape[0]
    parts = lax.axis_size("head")
    shard, part = lax.axis_index("seq"), lax.axis_index("head")
    z, x = shard // INNER, shard % INNER
    for k in range(outer):
        first = ((z ^ k) * parts + part) * share
        outs[k][...] = cot_ref[:, pl.ds(pl.multiple_of(first, 128), share)].T
    tok = bias_ref.shape[1]
    row = lax.broadcasted_iota(jnp.int32, (tok, tok), 0)
    lane = lax.broadcasted_iota(jnp.int32, (tok, tok), 1)
    for e in range(INNER):
        place = z * INNER + (x + e) % INNER
        qpos = place * tok + row
        begin = jnp.zeros((tok, tok), jnp.int32)
        end = jnp.int32(0)
        for i in range(lengths_ref.shape[1]):
            end = end + lengths_ref[0, i]
            begin = jnp.where(qpos >= end, jnp.maximum(begin, end), begin)
        for i, hop in enumerate((0, 2, 1)):
            kpos = (place - hop) * tok + lane
            allowed = (kpos >= begin) & (kpos <= qpos)
            bias_ref[e, :, i * tok:(i + 1) * tok] = jnp.where(allowed, 0.0, -1e30).astype(F32)


def join_kernel(*refs):
    out_ref = refs[-1]
    for i, piece in enumerate(refs[:-1]):
        tok = piece.shape[1]
        out_ref[:, i * tok:(i + 1) * tok] = piece[...]


def in_order(blocks, got_ref, x):
    tok, width = got_ref.shape[0], blocks[0].shape[1]
    out = []
    for group in range(INNER):
        for chunk, block in enumerate(blocks):
            out.append(jnp.where(x == group, block[:tok], got_ref[:, chunk * width:(chunk + 1) * width]))
    return out


def given_kernel(*refs):
    weights, out_ref = refs[CHUNKS + 1:-1], refs[-1]
    douts = in_order(refs[:CHUNKS], refs[CHUNKS], lax.axis_index("seq") % INNER)
    each = len(douts) // len(weights)
    out = None
    for i, weight in enumerate(weights):
        term = nn_dot(jnp.concatenate(douts[i * each:(i + 1) * each], axis=1), weight[...])
        out = term if out is None else out + term
    out_ref[...] = out.astype(out_ref.dtype)


def kept_kernel(*refs):
    weight_ref, other_ref, out_ref, near_weight, sems = refs[CHUNKS + 1:]
    cols = near_weight.shape[1]
    span = pl.ds(pl.multiple_of(lax.axis_index("head") * cols, 128), cols)
    fetches = start_rows(weight_ref, 0, span, near_weight, sems)
    douts = in_order(refs[:CHUNKS], refs[CHUNKS], lax.axis_index("seq") % INNER)
    count, width = len(douts), douts[0].shape[1]
    out = other_ref[...].astype(F32)
    for i, dout in enumerate(douts):
        for fetch in fetches[i * len(fetches) // count:(i + 1) * len(fetches) // count]:
            fetch.wait()
        out = out + nn_dot(dout, near_weight[i * width:(i + 1) * width, :])
    out_ref[...] = out.astype(out_ref.dtype)


def product_kernel(shifts, *refs):
    cots = refs[:2 * INNER]
    all_ref = refs[-1]
    pieces, outs = refs[2 * INNER:-len(shifts) - 1], refs[-len(shifts) - 1:-1]
    count = lax.axis_size("dp")
    x, own, part = lax.axis_index("seq") % INNER, lax.axis_index("dp"), lax.axis_index("head")
    tok = pieces[0].shape[0] // INNER
    douts = [p[e * tok:(e + 1) * tok] for e in range(INNER) for p in pieces]
    dout = jnp.concatenate(douts, axis=0)
    rows = outs[0].shape[0]
    half = cots[0].shape[0]
    for i in range(2):
        cot = jnp.concatenate([c[...] for c in cots[i * INNER:(i + 1) * INNER]], axis=1)
        at = pl.multiple_of(((part + i) % 2) * half, 128)
        all_ref[pl.ds(at, half), :] = nn_dot(cot, dout)
    for (dx, dy), out in zip(shifts, outs):
        at = pl.multiple_of((((x + dx) % INNER) * count + (own + dy) % count) * rows, 16)
        out[...] = all_ref[pl.ds(at, rows), :].astype(out.dtype)


def finish_kernel(*refs):
    refs, (out_ref, near_out, sems) = refs[:-3], refs[-3:]
    each = len(refs) // CHUNKS
    copies = []
    x = lax.axis_index("seq") % INNER
    span = out_ref.shape[1] // INNER
    for j in range(CHUNKS):
        mine = refs[j * each:(j + 1) * each]
        side = each // INNER
        for dx in range(INNER):
            out = mine[dx * side][...].astype(F32)
            for other in mine[dx * side + 1:(dx + 1) * side]:
                out = out + other[...].astype(F32)
            width = out.shape[1]
            group = (x - dx) % INNER
            at = pl.multiple_of(group * span + j * width, 128)
            slot = j * INNER + dx
            near_out[slot] = out
            copies.append(pltpu.make_async_copy(near_out.at[slot], out_ref.at[:, pl.ds(at, width)], sems.at[slot]))
            copies[-1].start()
    for copy in copies:
        copy.wait()


def on_device(queries, keys, values, query_tangent, key_tangent, value_tangent, lengths, out_weight, cotangent):
    tok = queries.shape[1]
    seq_count, dp_count, head_count = (lax.axis_size(a) for a in ("seq", "dp", "head"))
    outer = seq_count // INNER
    groups = keys.shape[2] // HEAD_DIM
    width = queries.shape[2] // groups
    model = out_weight.shape[1]
    assert groups == INNER and head_count == INNER

    def call(kernel, shapes, *args, given=0, scratch=()):
        args = args[:given] + tuple(near(a) for a in args[given:])
        return pl.pallas_call(
            kernel,
            out_shape=[VMEM(*s) if isinstance(s, tuple) else s for s in shapes],
            in_specs=specs(len(args)),
            out_specs=specs(len(shapes)),
            scratch_shapes=scratch,
            compiler_params=PARAMS,
        )(*args)

    def outward(block, k):
        return lax.ppermute(block, "seq", [(i, i ^ (k * INNER)) for i in range(seq_count)])

    def across(block):
        return lax.ppermute(block, "seq", [(i, i // INNER * INNER + (i + 1) % INNER) for i in range(seq_count)])

    def aside(block, s):
        return lax.ppermute(block, "head", [(i, (i + s) % head_count) for i in range(head_count)])

    def to_owner(block, dx, dy):
        perm = []
        for i in range(seq_count):
            for d in range(dp_count):
                to = i // INNER * INNER + (i + dx) % INNER
                perm.append((i * dp_count + d, to * dp_count + (d + dy) % dp_count))
        return lax.ppermute(block, ("seq", "dp"), perm)

    kv_shape = ((4, tok, HEAD_DIM), BF16)
    own_kv, give_kv = call(
        pack_kernel, [kv_shape] * 2, *(far(a[0]) for a in (keys, values, key_tangent, value_tangent)), given=4
    )
    other_kv = across(give_kv)
    hop = [(i, (i + INNER) % seq_count) for i in range(seq_count)]
    own_back = lax.ppermute(own_kv, "seq", hop)
    other_back = lax.ppermute(other_kv, "seq", hop)
    q_shape = ((2, tok, width), BF16)
    own_q, give_q = call(pack_queries_kernel, [q_shape] * 2, far(queries[0]), far(query_tangent[0]), given=2)
    other_q = across(give_q)

    share = model // (outer * head_count)
    *turned, bias = pl.pallas_call(
        turn_kernel,
        out_shape=[VMEM((share, tok), BF16)] * outer + [VMEM((INNER, tok, tok * (DOC_SHARDS + 1)), F32)],
        in_specs=[pl.BlockSpec(memory_space=pltpu.SMEM)] + specs(1),
        out_specs=specs(outer + 1),
        compiler_params=PARAMS,
        name="turn",
    )(far(lengths), far(cotangent[0]))
    arrived = [turned[0]] + [outward(turned[k], k) for k in range(1, outer)]
    beside = [across(block) for block in arrived]
    joined = ((share, tok * outer), BF16)
    cots = [call(join_kernel, [joined], *blocks)[0] for blocks in (arrived, beside)]
    cots += [aside(cot, 1) for cot in cots]

    out_cols = model // head_count
    blocks, weights, give = [], [], []
    for j in range(CHUNKS):
        inputs = [bias, own_q, other_q, out_weight, own_kv, other_kv, own_back, other_back, *give]
        block, given_dout, near_weight = pl.pallas_call(
            functools.partial(attend_kernel, j),
            out_shape=[
                VMEM((INNER * tok, width // CHUNKS), BF16),
                VMEM((tok, width), BF16),
                VMEM((width * groups // CHUNKS, out_cols), BF16),
            ],
            in_specs=specs(3) + [pl.BlockSpec(memory_space=pltpu.HBM)] + specs(len(inputs) - 4),
            out_specs=specs(3),
            scratch_shapes=[pltpu.SemaphoreType.DMA((4,))],
            compiler_params=PARAMS,
        )(*(far(a) if i == 3 else near(a) for i, a in enumerate(inputs)))
        blocks.append(block)
        weights.append(near_weight)
        give = [given_dout]
    got = across(give[0])

    def gather(block):
        held = {0: block}
        step = outer // 2
        while step:
            held.update({k + step: outward(b, step) for k, b in held.items()})
            step //= 2
        return [held[k] for k in range(outer)]

    pieces = [gather(block) for block in blocks]

    (given,) = call(given_kernel, [((tok, out_cols), BF16)], *blocks, got, *weights)
    added = aside(given, 1)
    layer_tangent = pl.pallas_call(
        kept_kernel,
        out_shape=jax.ShapeDtypeStruct((tok, out_cols), BF16),
        in_specs=specs(CHUNKS + 1) + [pl.BlockSpec(memory_space=pltpu.HBM)] + specs(1),
        out_specs=specs(1)[0],
        scratch_shapes=[VMEM((width * groups, out_cols), BF16), pltpu.SemaphoreType.DMA((8,))],
        compiler_params=PARAMS,
        name="kept",
    )(*(near(b) for b in (*blocks, got)), far(out_weight), near(added))

    rows = model // (seq_count * dp_count)
    order = [(dx, dy) for dx in reversed(range(INNER)) for dy in reversed(range(dp_count)) if dx or dy]
    parts = []
    for j in range(CHUNKS):
        shape = (rows, width // CHUNKS)
        *sent, mine = call(
            functools.partial(product_kernel, order + [(0, 0)]),
            [(shape, BF16)] * len(order) + [(shape, F32)],
            *cots,
            *pieces[j],
            scratch=[VMEM((share * head_count, width // CHUNKS), F32)],
        )
        came = {at: to_owner(block, *at) for at, block in zip(order, sent)}
        came[(0, 0)] = mine
        parts += [came[(dx, dy)] for dx in range(INNER) for dy in range(dp_count)]
    slots = CHUNKS * INNER
    weight_hvp = pl.pallas_call(
        finish_kernel,
        out_shape=jax.ShapeDtypeStruct((rows, width * groups), F32),
        in_specs=specs(len(parts)),
        out_specs=pl.BlockSpec(memory_space=pltpu.HBM),
        scratch_shapes=[VMEM((slots, rows, width // CHUNKS), F32), pltpu.SemaphoreType.DMA((slots,))],
        compiler_params=PARAMS,
        name="finish",
    )(*(near(p) for p in parts))
    return (layer_tangent[None], weight_hvp)


def solution(mesh):
    placed = (
        P("dp", "seq", "head"),
        P("dp", "seq", "head"),
        P("dp", "seq", "head"),
        P("dp", "seq", "head"),
        P("dp", "seq", "head"),
        P("dp", "seq", "head"),
        P("dp", None),
        P("head", None),
        P("dp", "seq", None),
    )

    return jax.shard_map(
        on_device,
        mesh=mesh,
        in_specs=placed,
        out_specs=(P("dp", "seq", "head"), P(("seq", "dp"), "head")),
        check_vma=False,
    )
```
